512 devices in a mesh: blk: 16 (over x, y_lo), neg: 32 (over z, y_hi, core).
Axes of the slice: x: 4, y: 8 (y_hi: 2, y_lo: 4; y = y_hi * 4 + y_lo), z: 8, core: 2. Of those that a mesh axis runs over, the one named last changes fastest.
Arguments:
- queries: bfloat16 [65536, 768], P(('blk', 'neg')), may hold values from -12 to 12
- passages: bfloat16 [65536, 768], P(('blk', 'neg')), may hold values from -3 to 3
- positive: int32 [65536], P(('blk', 'neg')), may hold values from 0 to 127
- hard_owner: int32 [16, 4], P('blk'), may hold values from 0 to 31
- hard_block: int32 [16, 4], P('blk'), may hold values from 0 to 7
- hard_pick: int32 [1024, 2], P(('blk', 'neg')), may hold values from 0 to 3, all different within a row
Outputs:
- loss: float32 [], replicated
- query_grad: bfloat16 [65536, 768], P(('blk', 'neg'))
- passage_grad: bfloat16 [65536, 768], P(('blk', 'neg'))
The draws below stay inside these ranges and needn't reach their ends.
Inputs may be any that keep to these rules, and one draw needn't show every extreme that they name: `hard_pick`: the 2 blocks of a query group differ.
All inputs are finite; a program needn't handle non-finite values.
Results may differ from the reference program's by a relative error of at most 0.014.
Values may be sent and summed in bfloat16 or wider, within the bound.
A program may use at most 64 MiB of HBM per device.

```python
import math
import jax
import jax.numpy as jnp
import numpy as np
from jax import lax

D = 768
ROWS_DEV = 128
STEPS = 1
H = 4
HB = 16
GQ = 64
K = 2
QUERIES = 65536
NBLK = 8
GROUPS = 1024
N_BLK = 16
N_NEG = 32


def drawn_rows(key, rows):
    values = jax.random.normal(key, (rows, D), jnp.float32)
    return jnp.clip(values, -3.0, 3.0)


def draw_queries(key, part):
    values = drawn_rows(jax.random.fold_in(key, 1), QUERIES)
    places = (jnp.arange(QUERIES) // ROWS_DEV).astype(jnp.float32)
    devices_total = QUERIES // ROWS_DEV
    rise = 1.0 + 2.0 * places / (devices_total - 1)
    values = values * rise[:, None]
    return values.astype(jnp.bfloat16)


def draw_passages(key, part):
    values = drawn_rows(jax.random.fold_in(key, 2), QUERIES)
    return values.astype(jnp.bfloat16)


def with_ends(entries, key, least, top_value):
    index_at = [jax.random.randint(jax.random.fold_in(key, axis), (), 0, length) for axis, length in enumerate(entries.shape)]
    widest = entries.shape.index(max(entries.shape))
    neighbour = index_at[:widest] + [(index_at[widest] + 1) % entries.shape[widest]] + index_at[widest + 1:]
    return entries.at[tuple(index_at)].set(least).at[tuple(neighbour)].set(top_value)


def rank_table(count, lean):
    portions = [(1 << 20) // math.isqrt(grade ** lean) + 1 for grade in range(1, count + 1)]
    deviation = 1 + sum(portions) // (1 << 30)
    return np.cumsum(np.array([max(1, weight // deviation) for weight in portions]))


def ranked(own_key, extent, amount, lean):
    table = rank_table(amount, lean)
    lot = jax.random.randint(jax.random.fold_in(own_key, 1), extent, 0, int(table[amount - 1]))
    standing = jnp.searchsorted(jnp.asarray(table, jnp.int32), lot, side="right")
    return jax.random.permutation(jax.random.fold_in(own_key, 2), amount)[standing].astype(jnp.int32)


def picks_of(stream_key, rows, amount, top, lift):
    sequence = jax.random.permutation(jax.random.fold_in(stream_key, 1), amount)
    boost = sequence
    for power in range(3):
        boost = boost * boost // amount
    boost = boost * lift // amount
    tickets = jax.random.randint(jax.random.fold_in(stream_key, 2), (rows, amount), 0, 4096) + boost
    holders = jax.random.permutation(jax.random.fold_in(stream_key, 3), rows)[jnp.arange(amount) % rows]
    tickets = jnp.where(jnp.arange(rows)[:, None] == holders[None, :], 1 << 14, tickets)
    merit = tickets * amount + jnp.arange(amount)
    return lax.top_k(merit.astype(jnp.int32), top)[1].astype(jnp.int32)


def setup_inputs(seed: int = 0) -> dict:
    key_of = jax.random.split(jax.random.key(seed), 7)
    return {
        "queries": draw_queries(jax.random.fold_in(key_of[6], 71), 0),
        "passages": draw_passages(jax.random.fold_in(key_of[6], 71), 0),
        "positive": with_ends(jax.random.randint(key_of[2], (QUERIES,), 0, ROWS_DEV), jax.random.fold_in(key_of[2], 1), 0, ROWS_DEV - 1).astype(jnp.int32),
        "hard_owner": with_ends(ranked(key_of[3], (N_BLK, H), N_NEG, 2), jax.random.fold_in(key_of[3], 3), 0, N_NEG - 1).astype(jnp.int32),
        "hard_block": with_ends(jax.random.randint(key_of[4], (N_BLK, H), 0, NBLK), jax.random.fold_in(key_of[4], 1), 0, NBLK - 1).astype(jnp.int32),
        "hard_pick": picks_of(key_of[5], GROUPS, H, K, 8192),
    }


def reference(queries, passages, positive, hard_owner, hard_block, hard_pick):
    scale = D ** -0.5
    qs = queries.reshape(N_BLK, N_NEG, ROWS_DEV, D)
    ps = passages.reshape(N_BLK, N_NEG, ROWS_DEV, D)
    pslots = passages.reshape(N_BLK, N_NEG, NBLK, HB, D)
    pos_all = positive.reshape(N_BLK, N_NEG, ROWS_DEV)
    picks = hard_pick.reshape(N_BLK, N_NEG, ROWS_DEV // GQ, K)
    width = (STEPS + 1) * ROWS_DEV + H * HB

    def visit(index, carry):
        total, qgrad, pgrad = carry
        b = index // N_NEG
        n = index % N_NEG
        query = qs[b, n]
        cycle = [ps[(b - k) % N_BLK, n] for k in range(STEPS + 1)]
        hard = pslots[b][hard_owner[b], hard_block[b]].reshape(H * HB, D)
        cand = jnp.concatenate(cycle + [hard], axis=0)
        scores = jnp.dot(query, cand.T, preferred_element_type=jnp.float32) * scale
        allowed = jnp.any(picks[b, n][:, :, None] == jnp.arange(H)[None, None, :], axis=1)
        hard_mask = jnp.repeat(jnp.repeat(allowed, GQ, axis=0), HB, axis=1)
        mask = jnp.concatenate([jnp.ones((ROWS_DEV, (STEPS + 1) * ROWS_DEV), bool), hard_mask], axis=1)
        scores = jnp.where(mask, scores, -jnp.inf)
        top = jnp.max(scores, axis=1)
        lse = top + jnp.log(jnp.sum(jnp.exp(scores - top[:, None]), axis=1))
        pos = pos_all[b, n]
        spos = jnp.take_along_axis(scores, pos[:, None], axis=1)[:, 0]
        total = total + jnp.sum(lse - spos)
        onehot = (jnp.arange(width)[None, :] == pos[:, None])
        grad_s = (jnp.exp(scores - lse[:, None]) - onehot.astype(jnp.float32)).astype(jnp.bfloat16)
        qg = (jnp.dot(grad_s, cand, preferred_element_type=jnp.float32) * scale).astype(jnp.bfloat16)
        qgrad = qgrad.at[b, n].set(qg)
        dc = jnp.dot(grad_s.T, query, preferred_element_type=jnp.float32) * scale
        for k in range(STEPS + 1):
            piece = dc[k * ROWS_DEV:(k + 1) * ROWS_DEV].reshape(NBLK, HB, D)
            pgrad = pgrad.at[(b - k) % N_BLK, n].add(piece)
        hpiece = dc[(STEPS + 1) * ROWS_DEV:].reshape(H, HB, D)
        pgrad = pgrad.at[b, hard_owner[b], hard_block[b]].add(hpiece)
        return total, qgrad, pgrad

    start = (jnp.zeros((), jnp.float32), jnp.zeros((N_BLK, N_NEG, ROWS_DEV, D), jnp.bfloat16),
             jnp.zeros((N_BLK, N_NEG, NBLK, HB, D), jnp.float32))
    total, qgrad, pgrad = lax.fori_loop(0, N_BLK * N_NEG, visit, start)
    loss = total / QUERIES
    return loss, qgrad.reshape(QUERIES, D), pgrad.reshape(QUERIES, D).astype(jnp.bfloat16)
```

```python
import functools

import jax
import jax.numpy as jnp
from jax import lax
from jax.experimental import pallas as pl
from jax.experimental.pallas import tpu as pltpu
from jax.sharding import PartitionSpec as P

MESH = pl.DeviceIdType.MESH
H = 4
HB = 16
GQ = 64
NZ = 8
NX = 4
NYL = 4
ZORDER = (4, 3, 5, 2, 6, 1, 7)


def nt(a, b):
    return lax.dot_general(a, b, (((1,), (1,)), ((), ())), preferred_element_type=jnp.float32)


def nn(a, b):
    return lax.dot_general(a, b, (((1,), (0,)), ((), ())), preferred_element_type=jnp.float32)


def tn(a, b):
    return lax.dot_general(a, b, (((0,), (0,)), ((), ())), preferred_element_type=jnp.float32)


def kernel(
    n_all,
    q_hbm, p_hbm, pos_ref, own_ref, blk_ref, pick_ref,
    loss_ref, qg_ref, pg_ref,
    qv, pv, cv, hv, fsend, frecv, fx, fxr,
    gsend, grecv, gx, gxr, gt, cgs, cgr, og,
    l1, l1r, l2, l2r, l3, l3r,
    lsem, ss, fr_s, fx_s, fa_s, gr_s, gx_s, ga_s, c_s, l1_s, l2_s, l3_s,
):
    blk = lax.axis_index("blk")
    neg = lax.axis_index("neg")
    rows, width = p_hbm.shape
    scale = width ** (-0.5)
    half = width // 2
    z = neg // 4
    yh = (neg // 2) % 2
    core = neg % 2
    x = blk // NYL
    yl = blk % NYL
    y = yh * NYL + yl

    zpeer = {d: {"blk": blk, "neg": ((z + d) % NZ) * 4 + yh * 2 + core} for d in range(1, NZ)}
    ypeer = {
        d: {
            "blk": x * NYL + ((y + d) % 8) % NYL,
            "neg": z * 4 + (((y + d) % 8) // NYL) * 2 + core,
        }
        for d in range(1, 8)
    }
    xpeer = {}
    for d in range(1, 8):
        xpeer[d] = {
            "blk": ((x + d // 2) % NX) * NYL + yl,
            "neg": z * 4 + yh * 2 + (core + d % 2) % 2,
        }
    mpeer = {
        d: {"blk": blk, "neg": z * 4 + ((yh + d // 2) % 2) * 2 + (core + d % 2) % 2}
        for d in range(1, 4)
    }
    after = {"blk": (blk + 1) % 16, "neg": neg}
    before = {"blk": (blk + 15) % 16, "neg": neg}

    load_p = pltpu.make_async_copy(p_hbm, pv, lsem.at[0])
    load_q = pltpu.make_async_copy(q_hbm, qv, lsem.at[1])
    load_p.start()
    load_q.start()

    barrier = pltpu.get_barrier_semaphore()
    greet = list(zpeer.values()) + list(ypeer.values()) + list(xpeer.values())
    greet += [mpeer[3], after, before]
    for who in greet:
        pl.semaphore_signal(barrier, inc=1, device_id=who, device_id_type=MESH)

    srow = lax.broadcasted_iota(jnp.int32, (H * HB, rows), 0)
    owner = jnp.zeros_like(srow)
    place = jnp.zeros_like(srow)
    for h in range(H):
        owner = jnp.where(srow // HB == h, own_ref[:, h:h + 1], owner)
        place = jnp.where(srow // HB == h, blk_ref[:, h:h + 1], place)
    chosen = (owner == neg) & (place * HB + srow % HB == lax.broadcasted_iota(jnp.int32, srow.shape, 1))
    sel = chosen.astype(jnp.float32).astype(jnp.bfloat16)
    load_p.wait()
    fsend[...] = nn(sel, pv[...]).astype(jnp.bfloat16)
    pl.semaphore_wait(barrier, len(greet))

    sent = []

    def push(src, dst, send, recv, who):
        copy = pltpu.make_async_remote_copy(
            src_ref=src, dst_ref=dst, send_sem=send, recv_sem=recv,
            device_id=who, device_id_type=MESH,
        )
        copy.start()
        sent.append(copy)
        return copy

    def part(ref, index):
        return ref.at[
            pl.ds(pl.multiple_of((index // 2) * HB, HB), HB),
            pl.ds(pl.multiple_of((index % 2) * half, half), half),
        ]

    sends = iter(range(64))

    def scatter(buf, land, sem):
        return [
            push(part(buf, (z + d) % NZ), land.at[d - 1], ss.at[next(sends)], sem.at[d - 1], zpeer[d])
            for d in ZORDER
        ]

    def gather(buf, sem):
        return [
            push(part(buf, z), part(buf, z), ss.at[next(sends)], sem.at[d - 1], zpeer[d])
            for d in ZORDER
        ]

    def middle(buf, land, sem):
        return [
            push(buf, land.at[d - 1], ss.at[next(sends)], sem.at[d - 1], mpeer[d]) for d in (3, 2, 1)
        ]

    def arrive(copies):
        for copy in copies:
            copy.wait_recv()

    def load_part(ref):
        return part(ref, z)[...].astype(jnp.float32)

    f1 = scatter(fsend, frecv, fr_s)
    cyc = push(pv, cv, ss.at[next(sends)], c_s.at[0], after)

    load_q.wait()
    q = qv[...]
    s0 = nt(pv[...], q) * scale

    arrive(f1)
    fx[...] = (load_part(fsend) + jnp.sum(frecv[...].astype(jnp.float32), axis=0)).astype(jnp.bfloat16)
    f2 = middle(fx, fxr, fx_s)
    arrive(f2)
    part(hv, z)[...] = (
        fx[...].astype(jnp.float32) + jnp.sum(fxr[...].astype(jnp.float32), axis=0)
    ).astype(jnp.bfloat16)
    f3 = gather(hv, fa_s)
    cyc.wait_recv()
    s1 = nt(cv[...], q) * scale
    arrive(f3)
    s2 = nt(hv[...], q) * scale

    lane = lax.broadcasted_iota(jnp.int32, s2.shape, 1)
    slot = lax.broadcasted_iota(jnp.int32, s2.shape, 0) // HB
    first = jnp.where(lane < GQ, pick_ref[0:1, 0:1], pick_ref[1:2, 0:1])
    second = jnp.where(lane < GQ, pick_ref[0:1, 1:2], pick_ref[1:2, 1:2])
    s2 = jnp.where((slot == first) | (slot == second), s2, -jnp.inf)
    top = jnp.maximum(
        jnp.maximum(jnp.max(s0, axis=0, keepdims=True), jnp.max(s1, axis=0, keepdims=True)),
        jnp.max(s2, axis=0, keepdims=True),
    )
    total = (
        jnp.sum(jnp.exp(s0 - top), axis=0, keepdims=True)
        + jnp.sum(jnp.exp(s1 - top), axis=0, keepdims=True)
        + jnp.sum(jnp.exp(s2 - top), axis=0, keepdims=True)
    )
    lse = top + jnp.log(total)
    hot = lax.broadcasted_iota(jnp.int32, s0.shape, 0) == pos_ref[...]

    g2 = jnp.exp(s2 - lse).astype(jnp.bfloat16)
    gsend[...] = (nn(g2, q) * scale).astype(jnp.bfloat16)
    b1 = scatter(gsend, grecv, gr_s)

    l1[...] = lse - jnp.sum(jnp.where(hot, s0, 0.0), axis=0, keepdims=True)
    a1 = [push(l1, l1r.at[d - 1], ss.at[next(sends)], l1_s.at[d - 1], zpeer[d]) for d in ZORDER]

    g1 = jnp.exp(s1 - lse).astype(jnp.bfloat16)
    cgs[...] = (nn(g1, q) * scale).astype(jnp.bfloat16)
    back = push(cgs, cgr, ss.at[next(sends)], c_s.at[1], before)

    g0 = (jnp.exp(s0 - lse) - hot.astype(jnp.float32)).astype(jnp.bfloat16)
    og[...] = nn(g0, q) * scale
    qg_ref[...] = ((tn(g0, pv[...]) + tn(g1, cv[...]) + tn(g2, hv[...])) * scale).astype(jnp.bfloat16)

    arrive(b1)
    gx[...] = (load_part(gsend) + jnp.sum(grecv[...].astype(jnp.float32), axis=0)).astype(jnp.bfloat16)
    b2 = middle(gx, gxr, gx_s)
    arrive(a1)
    l2[...] = l1[...] + jnp.sum(l1r[...], axis=0)
    a2 = [push(l2, l2r.at[d - 1], ss.at[next(sends)], l2_s.at[d - 1], ypeer[d]) for d in ZORDER]
    arrive(b2)
    part(gt, z)[...] = (
        gx[...].astype(jnp.float32) + jnp.sum(gxr[...].astype(jnp.float32), axis=0)
    ).astype(jnp.bfloat16)
    b3 = gather(gt, ga_s)
    arrive(a2)
    l3[...] = l2[...] + jnp.sum(l2r[...], axis=0)
    a3 = [push(l3, l3r.at[d - 1], ss.at[next(sends)], l3_s.at[d - 1], xpeer[d]) for d in range(1, 8)]
    back.wait_recv()
    og[...] += cgr[...].astype(jnp.float32)
    arrive(a3)
    loss_ref[0, 0] = jnp.sum(l3[...] + jnp.sum(l3r[...], axis=0)) / n_all
    arrive(b3)
    pg_ref[...] = (og[...] + tn(sel, gt[...])).astype(jnp.bfloat16)
    for copy in sent:
        copy.wait_send()


def body(queries, passages, positive, hard_owner, hard_block, hard_pick):
    rows, width = passages.shape
    n_all = rows * lax.axis_size("blk") * lax.axis_size("neg")
    bf = jnp.bfloat16
    f32 = jnp.float32
    any_space = pl.BlockSpec(memory_space=pl.ANY)
    vmem = pl.BlockSpec(memory_space=pltpu.VMEM)
    smem = pl.BlockSpec(memory_space=pltpu.SMEM)
    half = width // 2
    dma = pltpu.SemaphoreType.DMA
    loss, query_grad, passage_grad = pl.pallas_call(
        functools.partial(kernel, n_all),
        out_shape=(
            jax.ShapeDtypeStruct((1, 1), f32),
            jax.ShapeDtypeStruct((rows, width), bf),
            jax.ShapeDtypeStruct((rows, width), bf),
        ),
        in_specs=[any_space, any_space, vmem, vmem, vmem, vmem],
        out_specs=(smem, vmem, vmem),
        scratch_shapes=[
            pltpu.VMEM((rows, width), bf),
            pltpu.VMEM((rows, width), bf),
            pltpu.VMEM((rows, width), bf),
            pltpu.VMEM((H * HB, width), bf),
            pltpu.VMEM((H * HB, width), bf),
            pltpu.VMEM((NZ - 1, HB, half), bf),
            pltpu.VMEM((HB, half), bf),
            pltpu.VMEM((3, HB, half), bf),
            pltpu.VMEM((H * HB, width), bf),
            pltpu.VMEM((NZ - 1, HB, half), bf),
            pltpu.VMEM((HB, half), bf),
            pltpu.VMEM((3, HB, half), bf),
            pltpu.VMEM((H * HB, width), bf),
            pltpu.VMEM((rows, width), bf),
            pltpu.VMEM((rows, width), bf),
            pltpu.VMEM((rows, width), f32),
            pltpu.VMEM((1, rows), f32),
            pltpu.VMEM((7, 1, rows), f32),
            pltpu.VMEM((1, rows), f32),
            pltpu.VMEM((7, 1, rows), f32),
            pltpu.VMEM((1, rows), f32),
            pltpu.VMEM((7, 1, rows), f32),
            dma((2,)),
            dma((64,)),
            dma((NZ - 1,)),
            dma((3,)),
            dma((NZ - 1,)),
            dma((NZ - 1,)),
            dma((3,)),
            dma((NZ - 1,)),
            dma((2,)),
            dma((7,)),
            dma((7,)),
            dma((7,)),
        ],
        compiler_params=pltpu.CompilerParams(collective_id=0, has_side_effects=True),
        name="retriever",
    )(queries, passages, positive.reshape(1, rows), hard_owner, hard_block, hard_pick)
    return (loss[0, 0], query_grad, passage_grad)


def solution(mesh):
    placed = (
        P(("blk", "neg"), None),
        P(("blk", "neg"), None),
        P(("blk", "neg")),
        P("blk", None),
        P("blk", None),
        P(("blk", "neg"), None),
    )
    return jax.shard_map(
        body,
        mesh=mesh,
        in_specs=placed,
        out_specs=(P(), P(("blk", "neg"), None), P(("blk", "neg"), None)),
        check_vma=False,
    )
```

```python
import functools

import jax
import jax.numpy as jnp
from jax import lax
from jax.experimental import pallas as pl
from jax.experimental.pallas import tpu as pltpu
from jax.sharding import PartitionSpec as P

MESH = pl.DeviceIdType.MESH
H = 4
HB = 16
GQ = 64
NZ = 8
NX = 4
NYL = 4
ZORDER = (4, 3, 5, 2, 6, 1, 7)


def nt(a, b):
    return lax.dot_general(a, b, (((1,), (1,)), ((), ())), preferred_element_type=jnp.float32)


def nn(a, b):
    return lax.dot_general(a, b, (((1,), (0,)), ((), ())), preferred_element_type=jnp.float32)


def tn(a, b):
    return lax.dot_general(a, b, (((0,), (0,)), ((), ())), preferred_element_type=jnp.float32)


def kernel(
    n_all,
    q_hbm, p_hbm, pos_hbm, own_hbm, blk_hbm, pick_hbm,
    loss_ref, out_ref,
    pos_ref, own_ref, blk_ref, pick_ref,
    qv, pv, cv, hv, fsend, frecv, fx, fxr,
    gsend, grecv, gx, gxr, gt, cgs, cgr, og,
    l1, l1r, l2, l2r, l3, l3r,
    lsem, ss, fr_s, fx_s, fa_s, gr_s, gx_s, ga_s, c_s, l1_s, l2_s, l3_s,
):
    blk = lax.axis_index("blk")
    neg = lax.axis_index("neg")
    rows, width = p_hbm.shape
    scale = width ** (-0.5)
    half = width // 2
    z = neg // 4
    yh = (neg // 2) % 2
    core = neg % 2
    x = blk // NYL
    yl = blk % NYL
    y = yh * NYL + yl

    zpeer = {d: {"blk": blk, "neg": ((z + d) % NZ) * 4 + yh * 2 + core} for d in range(1, NZ)}
    ypeer = {
        d: {
            "blk": x * NYL + ((y + d) % 8) % NYL,
            "neg": z * 4 + (((y + d) % 8) // NYL) * 2 + core,
        }
        for d in range(1, 8)
    }
    xpeer = {}
    for d in range(1, 8):
        xpeer[d] = {
            "blk": ((x + d // 2) % NX) * NYL + yl,
            "neg": z * 4 + yh * 2 + (core + d % 2) % 2,
        }
    mpeer = {
        d: {"blk": blk, "neg": z * 4 + ((yh + d // 2) % 2) * 2 + (core + d % 2) % 2}
        for d in range(1, 4)
    }
    after = {"blk": (blk + 1) % 16, "neg": neg}
    before = {"blk": (blk + 15) % 16, "neg": neg}

    load_p = pltpu.make_async_copy(p_hbm, pv, lsem.at[0])
    load_q = pltpu.make_async_copy(q_hbm, qv, lsem.at[1])
    load_own = pltpu.make_async_copy(own_hbm, own_ref, lsem.at[2])
    load_blk = pltpu.make_async_copy(blk_hbm, blk_ref, lsem.at[3])
    load_pos = pltpu.make_async_copy(pos_hbm, pos_ref, lsem.at[4])
    load_pick = pltpu.make_async_copy(pick_hbm, pick_ref, lsem.at[5])
    load_p.start()
    load_own.start()
    load_blk.start()
    load_q.start()
    load_pos.start()
    load_pick.start()

    barrier = pltpu.get_barrier_semaphore()
    greet = list(zpeer.values()) + list(ypeer.values()) + list(xpeer.values())
    greet += [mpeer[3], after, before]
    for who in greet:
        pl.semaphore_signal(barrier, inc=1, device_id=who, device_id_type=MESH)

    load_own.wait()
    load_blk.wait()
    srow = lax.broadcasted_iota(jnp.int32, (H * HB, rows), 0)
    owner = jnp.zeros_like(srow)
    place = jnp.zeros_like(srow)
    for h in range(H):
        owner = jnp.where(srow // HB == h, own_ref[:, h:h + 1], owner)
        place = jnp.where(srow // HB == h, blk_ref[:, h:h + 1], place)
    chosen = (owner == neg) & (place * HB + srow % HB == lax.broadcasted_iota(jnp.int32, srow.shape, 1))
    sel = chosen.astype(jnp.float32).astype(jnp.bfloat16)
    load_p.wait()
    fsend[...] = nn(sel, pv[...]).astype(jnp.bfloat16)
    pl.semaphore_wait(barrier, len(greet))

    sent = []

    def push(src, dst, send, recv, who):
        copy = pltpu.make_async_remote_copy(
            src_ref=src, dst_ref=dst, send_sem=send, recv_sem=recv,
            device_id=who, device_id_type=MESH,
        )
        copy.start()
        sent.append(copy)
        return copy

    def part(ref, index):
        return ref.at[
            pl.ds(pl.multiple_of((index // 2) * HB, HB), HB),
            pl.ds(pl.multiple_of((index % 2) * half, half), half),
        ]

    sends = iter(range(64))

    def scatter(buf, land, sem):
        return [
            push(part(buf, (z + d) % NZ), land.at[d - 1], ss.at[next(sends)], sem.at[d - 1], zpeer[d])
            for d in ZORDER
        ]

    def gather(buf, sem):
        return [
            push(part(buf, z), part(buf, z), ss.at[next(sends)], sem.at[d - 1], zpeer[d])
            for d in ZORDER
        ]

    def middle(buf, land, sem):
        return [
            push(buf, land.at[d - 1], ss.at[next(sends)], sem.at[d - 1], mpeer[d]) for d in (3, 2, 1)
        ]

    def arrive(copies):
        for copy in copies:
            copy.wait_recv()

    def load_part(ref):
        return part(ref, z)[...].astype(jnp.float32)

    f1 = scatter(fsend, frecv, fr_s)
    cyc = push(pv, cv, ss.at[next(sends)], c_s.at[0], after)

    load_q.wait()
    load_pos.wait()
    load_pick.wait()
    q = qv[...]
    s0 = nt(pv[...], q) * scale

    arrive(f1)
    fx[...] = (load_part(fsend) + jnp.sum(frecv[...].astype(jnp.float32), axis=0)).astype(jnp.bfloat16)
    f2 = middle(fx, fxr, fx_s)
    arrive(f2)
    part(hv, z)[...] = (
        fx[...].astype(jnp.float32) + jnp.sum(fxr[...].astype(jnp.float32), axis=0)
    ).astype(jnp.bfloat16)
    f3 = gather(hv, fa_s)
    cyc.wait_recv()
    s1 = nt(cv[...], q) * scale
    arrive(f3)
    s2 = nt(hv[...], q) * scale

    lane = lax.broadcasted_iota(jnp.int32, s2.shape, 1)
    slot = lax.broadcasted_iota(jnp.int32, s2.shape, 0) // HB
    first = jnp.where(lane < GQ, pick_ref[0:1, 0:1], pick_ref[1:2, 0:1])
    second = jnp.where(lane < GQ, pick_ref[0:1, 1:2], pick_ref[1:2, 1:2])
    s2 = jnp.where((slot == first) | (slot == second), s2, -jnp.inf)
    top = jnp.maximum(
        jnp.maximum(jnp.max(s0, axis=0, keepdims=True), jnp.max(s1, axis=0, keepdims=True)),
        jnp.max(s2, axis=0, keepdims=True),
    )
    total = (
        jnp.sum(jnp.exp(s0 - top), axis=0, keepdims=True)
        + jnp.sum(jnp.exp(s1 - top), axis=0, keepdims=True)
        + jnp.sum(jnp.exp(s2 - top), axis=0, keepdims=True)
    )
    lse = top + jnp.log(total)
    hot = lax.broadcasted_iota(jnp.int32, s0.shape, 0) == pos_ref[...]

    g2 = jnp.exp(s2 - lse).astype(jnp.bfloat16)
    gsend[...] = (nn(g2, q) * scale).astype(jnp.bfloat16)
    b1 = scatter(gsend, grecv, gr_s)

    l1[...] = lse - jnp.sum(jnp.where(hot, s0, 0.0), axis=0, keepdims=True)
    a1 = [push(l1, l1r.at[d - 1], ss.at[next(sends)], l1_s.at[d - 1], zpeer[d]) for d in ZORDER]

    g1 = jnp.exp(s1 - lse).astype(jnp.bfloat16)
    cgs[...] = (nn(g1, q) * scale).astype(jnp.bfloat16)
    back = push(cgs, cgr, ss.at[next(sends)], c_s.at[1], before)

    g0 = (jnp.exp(s0 - lse) - hot.astype(jnp.float32)).astype(jnp.bfloat16)
    og[...] = nn(g0, q) * scale
    out_ref[0] = ((tn(g0, pv[...]) + tn(g1, cv[...]) + tn(g2, hv[...])) * scale).astype(jnp.bfloat16)

    arrive(b1)
    gx[...] = (load_part(gsend) + jnp.sum(grecv[...].astype(jnp.float32), axis=0)).astype(jnp.bfloat16)
    b2 = middle(gx, gxr, gx_s)
    arrive(a1)
    l2[...] = l1[...] + jnp.sum(l1r[...], axis=0)
    a2 = [push(l2, l2r.at[d - 1], ss.at[next(sends)], l2_s.at[d - 1], ypeer[d]) for d in ZORDER]
    arrive(b2)
    part(gt, z)[...] = (
        gx[...].astype(jnp.float32) + jnp.sum(gxr[...].astype(jnp.float32), axis=0)
    ).astype(jnp.bfloat16)
    b3 = gather(gt, ga_s)
    arrive(a2)
    l3[...] = l2[...] + jnp.sum(l2r[...], axis=0)
    a3 = [push(l3, l3r.at[d - 1], ss.at[next(sends)], l3_s.at[d - 1], xpeer[d]) for d in range(1, 8)]
    back.wait_recv()
    og[...] += cgr[...].astype(jnp.float32)
    arrive(a3)
    loss_ref[0, 0] = jnp.sum(l3[...] + jnp.sum(l3r[...], axis=0)) / n_all
    arrive(b3)
    out_ref[1] = (og[...] + tn(sel, gt[...])).astype(jnp.bfloat16)
    for copy in sent:
        copy.wait_send()


def body(queries, passages, positive, hard_owner, hard_block, hard_pick):
    rows, width = passages.shape
    n_all = rows * lax.axis_size("blk") * lax.axis_size("neg")
    bf = jnp.bfloat16
    f32 = jnp.float32
    any_space = pl.BlockSpec(memory_space=pl.ANY)
    vmem = pl.BlockSpec(memory_space=pltpu.VMEM)
    smem = pl.BlockSpec(memory_space=pltpu.SMEM)
    half = width // 2
    dma = pltpu.SemaphoreType.DMA
    loss, grads = pl.pallas_call(
        functools.partial(kernel, n_all),
        out_shape=(
            jax.ShapeDtypeStruct((1, 1), f32),
            pltpu.VMEM((2, rows, width), bf),
        ),
        in_specs=[any_space] * 6,
        out_specs=(smem, vmem),
        scratch_shapes=[
            pltpu.VMEM((1, rows), jnp.int32),
            pltpu.VMEM(hard_owner.shape, jnp.int32),
            pltpu.VMEM(hard_block.shape, jnp.int32),
            pltpu.VMEM(hard_pick.shape, jnp.int32),
            pltpu.VMEM((rows, width), bf),
            pltpu.VMEM((rows, width), bf),
            pltpu.VMEM((rows, width), bf),
            pltpu.VMEM((H * HB, width), bf),
            pltpu.VMEM((H * HB, width), bf),
            pltpu.VMEM((NZ - 1, HB, half), bf),
            pltpu.VMEM((HB, half), bf),
            pltpu.VMEM((3, HB, half), bf),
            pltpu.VMEM((H * HB, width), bf),
            pltpu.VMEM((NZ - 1, HB, half), bf),
            pltpu.VMEM((HB, half), bf),
            pltpu.VMEM((3, HB, half), bf),
            pltpu.VMEM((H * HB, width), bf),
            pltpu.VMEM((rows, width), bf),
            pltpu.VMEM((rows, width), bf),
            pltpu.VMEM((rows, width), f32),
            pltpu.VMEM((1, rows), f32),
            pltpu.VMEM((7, 1, rows), f32),
            pltpu.VMEM((1, rows), f32),
            pltpu.VMEM((7, 1, rows), f32),
            pltpu.VMEM((1, rows), f32),
            pltpu.VMEM((7, 1, rows), f32),
            dma((6,)),
            dma((64,)),
            dma((NZ - 1,)),
            dma((3,)),
            dma((NZ - 1,)),
            dma((NZ - 1,)),
            dma((3,)),
            dma((NZ - 1,)),
            dma((2,)),
            dma((7,)),
            dma((7,)),
            dma((7,)),
        ],
        compiler_params=pltpu.CompilerParams(collective_id=0, has_side_effects=True),
        name="retriever",
    )(queries, passages, positive.reshape(1, rows), hard_owner, hard_block, hard_pick)
    return (loss[0, 0], grads[0], grads[1])


def solution(mesh):
    placed = (
        P(("blk", "neg"), None),
        P(("blk", "neg"), None),
        P(("blk", "neg")),
        P("blk", None),
        P("blk", None),
        P(("blk", "neg"), None),
    )
    return jax.shard_map(
        body,
        mesh=mesh,
        in_specs=placed,
        out_specs=(P(), P(("blk", "neg"), None), P(("blk", "neg"), None)),
        check_vma=False,
    )
```

```python
import functools

import jax
import jax.numpy as jnp
from jax import lax
from jax.experimental import pallas as pl
from jax.experimental.pallas import tpu as pltpu
from jax.sharding import PartitionSpec as P

MESH = pl.DeviceIdType.MESH
H = 4
HB = 16
GQ = 64
NZ = 8
NX = 4
NYL = 4
ZORDER = (4, 3, 5, 2, 6, 1, 7)


def nt(a, b):
    return lax.dot_general(a, b, (((1,), (1,)), ((), ())), preferred_element_type=jnp.float32)


def nn(a, b):
    return lax.dot_general(a, b, (((1,), (0,)), ((), ())), preferred_element_type=jnp.float32)


def tn(a, b):
    return lax.dot_general(a, b, (((0,), (0,)), ((), ())), preferred_element_type=jnp.float32)


def kernel(
    n_all,
    q_hbm, p_hbm, pos_hbm, own_hbm, blk_hbm, pick_hbm,
    loss_ref, out_ref,
    pos_ref, own_ref, blk_ref, pick_ref,
    qv, pv, cv, hv, fsend, frecv, fx, fxr,
    gsend, grecv, gx, gxr, gt, cgs, cgr, og,
    l1, l1r, l2, l2r, l3, l3r,
    lsem, ss, fr_s, fx_s, fa_s, gr_s, gx_s, ga_s, c_s, l1_s, l2_s, l3_s,
):
    blk = lax.axis_index("blk")
    neg = lax.axis_index("neg")
    rows, width = p_hbm.shape
    scale = width ** (-0.5)
    half = width // 2
    z = neg // 4
    yh = (neg // 2) % 2
    core = neg % 2
    x = blk // NYL
    yl = blk % NYL
    y = yh * NYL + yl

    zpeer = {d: {"blk": blk, "neg": ((z + d) % NZ) * 4 + yh * 2 + core} for d in range(1, NZ)}
    ypeer = {
        d: {
            "blk": x * NYL + ((y + d) % 8) % NYL,
            "neg": z * 4 + (((y + d) % 8) // NYL) * 2 + core,
        }
        for d in range(1, 8)
    }
    xpeer = {}
    for d in range(1, 8):
        xpeer[d] = {
            "blk": ((x + d // 2) % NX) * NYL + yl,
            "neg": z * 4 + yh * 2 + (core + d % 2) % 2,
        }
    mpeer = {
        d: {"blk": blk, "neg": z * 4 + ((yh + d // 2) % 2) * 2 + (core + d % 2) % 2}
        for d in range(1, 4)
    }
    after = {"blk": (blk + 1) % 16, "neg": neg}
    before = {"blk": (blk + 15) % 16, "neg": neg}

    load_p = pltpu.make_async_copy(p_hbm, pv, lsem.at[0])
    load_q = pltpu.make_async_copy(q_hbm, qv, lsem.at[1])
    load_own = pltpu.make_async_copy(own_hbm, own_ref, lsem.at[2])
    load_blk = pltpu.make_async_copy(blk_hbm, blk_ref, lsem.at[3])
    load_pos = pltpu.make_async_copy(pos_hbm, pos_ref, lsem.at[4])
    load_pick = pltpu.make_async_copy(pick_hbm, pick_ref, lsem.at[5])
    load_p.start()
    load_own.start()
    load_blk.start()
    load_q.start()
    load_pos.start()
    load_pick.start()

    barrier = pltpu.get_barrier_semaphore()
    greet = list(zpeer.values()) + list(ypeer.values()) + list(xpeer.values())
    greet += [mpeer[3], after, before]
    for who in greet:
        pl.semaphore_signal(barrier, inc=1, device_id=who, device_id_type=MESH)

    load_own.wait()
    load_blk.wait()
    srow = lax.broadcasted_iota(jnp.int32, (H * HB, rows), 0)
    owner = jnp.zeros_like(srow)
    place = jnp.zeros_like(srow)
    for h in range(H):
        owner = jnp.where(srow // HB == h, own_ref[:, h:h + 1], owner)
        place = jnp.where(srow // HB == h, blk_ref[:, h:h + 1], place)
    chosen = (owner == neg) & (place * HB + srow % HB == lax.broadcasted_iota(jnp.int32, srow.shape, 1))
    sel = chosen.astype(jnp.float32).astype(jnp.bfloat16)
    load_p.wait()
    fsend[...] = nn(sel, pv[...]).astype(jnp.bfloat16)
    pl.semaphore_wait(barrier, len(greet))

    sent = []

    def push(src, dst, send, recv, who):
        copy = pltpu.make_async_remote_copy(
            src_ref=src, dst_ref=dst, send_sem=send, recv_sem=recv,
            device_id=who, device_id_type=MESH,
        )
        copy.start()
        sent.append(copy)
        return copy

    def leave():
        for copy in sent:
            copy.wait_send()
        sent.clear()

    def part(ref, index):
        return ref.at[
            pl.ds(pl.multiple_of((index // 2) * HB, HB), HB),
            pl.ds(pl.multiple_of((index % 2) * half, half), half),
        ]

    sends = iter(range(64))

    def scatter(buf, land, sem):
        return [
            push(part(buf, (z + d) % NZ), land.at[d - 1], ss.at[next(sends)], sem.at[d - 1], zpeer[d])
            for d in ZORDER
        ]

    def gather(buf, sem):
        return [
            push(part(buf, z), part(buf, z), ss.at[next(sends)], sem.at[d - 1], zpeer[d])
            for d in ZORDER
        ]

    def middle(buf, land, sem):
        return [
            push(buf, land.at[d - 1], ss.at[next(sends)], sem.at[d - 1], mpeer[d]) for d in (3, 2, 1)
        ]

    def arrive(copies):
        for copy in copies:
            copy.wait_recv()

    def load_part(ref):
        return part(ref, z)[...].astype(jnp.float32)

    f1 = scatter(fsend, frecv, fr_s)
    cyc = push(pv, cv, ss.at[next(sends)], c_s.at[0], after)

    scol = lax.broadcasted_iota(jnp.int32, (rows, H * HB), 1)
    owner_t = jnp.zeros_like(scol)
    place_t = jnp.zeros_like(scol)
    for h in range(H):
        owner_t = jnp.where(scol // HB == h, own_ref[:, h:h + 1], owner_t)
        place_t = jnp.where(scol // HB == h, blk_ref[:, h:h + 1], place_t)
    chosen_t = (owner_t == neg) & (
        place_t * HB + scol % HB == lax.broadcasted_iota(jnp.int32, scol.shape, 0)
    )
    sel_t = chosen_t.astype(jnp.float32).astype(jnp.bfloat16)
    load_q.wait()
    load_pos.wait()
    load_pick.wait()
    q = qv[...]
    s0 = nt(pv[...], q) * scale
    hot = lax.broadcasted_iota(jnp.int32, s0.shape, 0) == pos_ref[...]
    spos = jnp.sum(jnp.where(hot, s0, 0.0), axis=0, keepdims=True)

    arrive(f1)
    fx[...] = (load_part(fsend) + jnp.sum(frecv[...].astype(jnp.float32), axis=0)).astype(jnp.bfloat16)
    f2 = middle(fx, fxr, fx_s)
    arrive(f2)
    part(hv, z)[...] = (
        fx[...].astype(jnp.float32) + jnp.sum(fxr[...].astype(jnp.float32), axis=0)
    ).astype(jnp.bfloat16)
    f3 = gather(hv, fa_s)
    cyc.wait_recv()
    s1 = nt(cv[...], q) * scale
    top01 = jnp.maximum(jnp.max(s0, axis=0, keepdims=True), jnp.max(s1, axis=0, keepdims=True))
    sum01 = jnp.sum(jnp.exp(s0 - top01), axis=0, keepdims=True) + jnp.sum(
        jnp.exp(s1 - top01), axis=0, keepdims=True
    )
    lane = lax.broadcasted_iota(jnp.int32, (H * HB, rows), 1)
    slot = lax.broadcasted_iota(jnp.int32, (H * HB, rows), 0) // HB
    first = jnp.where(lane < GQ, pick_ref[0:1, 0:1], pick_ref[1:2, 0:1])
    second = jnp.where(lane < GQ, pick_ref[0:1, 1:2], pick_ref[1:2, 1:2])
    picked = (slot == first) | (slot == second)
    arrive(f3)
    s2 = nt(hv[...], q) * scale

    s2 = jnp.where(picked, s2, -jnp.inf)
    top = jnp.maximum(top01, jnp.max(s2, axis=0, keepdims=True))
    total = sum01 * jnp.exp(top01 - top) + jnp.sum(jnp.exp(s2 - top), axis=0, keepdims=True)
    lse = top + jnp.log(total)

    g2 = jnp.exp(s2 - lse).astype(jnp.bfloat16)
    gsend[...] = (nn(g2, q) * scale).astype(jnp.bfloat16)
    b1 = scatter(gsend, grecv, gr_s)

    l1[...] = lse - spos
    a1 = [push(l1, l1r.at[d - 1], ss.at[next(sends)], l1_s.at[d - 1], zpeer[d]) for d in ZORDER]

    g1 = jnp.exp(s1 - lse).astype(jnp.bfloat16)
    cgs[...] = (nn(g1, q) * scale).astype(jnp.bfloat16)
    back = push(cgs, cgr, ss.at[next(sends)], c_s.at[1], before)

    g0 = (jnp.exp(s0 - lse) - hot.astype(jnp.float32)).astype(jnp.bfloat16)
    og[...] = nn(g0, q) * scale
    out_ref[0] = ((tn(g0, pv[...]) + tn(g1, cv[...]) + tn(g2, hv[...])) * scale).astype(jnp.bfloat16)

    leave()
    arrive(b1)
    gx[...] = (load_part(gsend) + jnp.sum(grecv[...].astype(jnp.float32), axis=0)).astype(jnp.bfloat16)
    b2 = middle(gx, gxr, gx_s)
    arrive(a1)
    l2[...] = l1[...] + jnp.sum(l1r[...], axis=0)
    a2 = [push(l2, l2r.at[d - 1], ss.at[next(sends)], l2_s.at[d - 1], ypeer[d]) for d in ZORDER]
    arrive(b2)
    part(gt, z)[...] = (
        gx[...].astype(jnp.float32) + jnp.sum(gxr[...].astype(jnp.float32), axis=0)
    ).astype(jnp.bfloat16)
    b3 = gather(gt, ga_s)
    arrive(a2)
    l3[...] = l2[...] + jnp.sum(l2r[...], axis=0)
    a3 = [push(l3, l3r.at[d - 1], ss.at[next(sends)], l3_s.at[d - 1], xpeer[d]) for d in range(1, 8)]
    back.wait_recv()
    og[...] += cgr[...].astype(jnp.float32)
    arrive(a3)
    loss_ref[0, 0] = jnp.sum(l3[...] + jnp.sum(l3r[...], axis=0)) / n_all
    leave()
    arrive(b3)
    out_ref[1] = (og[...] + nn(sel_t, gt[...])).astype(jnp.bfloat16)


def body(queries, passages, positive, hard_owner, hard_block, hard_pick):
    rows, width = passages.shape
    n_all = rows * lax.axis_size("blk") * lax.axis_size("neg")
    bf = jnp.bfloat16
    f32 = jnp.float32
    any_space = pl.BlockSpec(memory_space=pl.ANY)
    vmem = pl.BlockSpec(memory_space=pltpu.VMEM)
    smem = pl.BlockSpec(memory_space=pltpu.SMEM)
    half = width // 2
    dma = pltpu.SemaphoreType.DMA
    loss, grads = pl.pallas_call(
        functools.partial(kernel, n_all),
        out_shape=(
            pltpu.SMEM((1, 1), f32),
            pltpu.VMEM((2, rows, width), bf),
        ),
        in_specs=[any_space] * 6,
        out_specs=(smem, vmem),
        scratch_shapes=[
            pltpu.VMEM((1, rows), jnp.int32),
            pltpu.VMEM(hard_owner.shape, jnp.int32),
            pltpu.VMEM(hard_block.shape, jnp.int32),
            pltpu.VMEM(hard_pick.shape, jnp.int32),
            pltpu.VMEM((rows, width), bf),
            pltpu.VMEM((rows, width), bf),
            pltpu.VMEM((rows, width), bf),
            pltpu.VMEM((H * HB, width), bf),
            pltpu.VMEM((H * HB, width), bf),
            pltpu.VMEM((NZ - 1, HB, half), bf),
            pltpu.VMEM((HB, half), bf),
            pltpu.VMEM((3, HB, half), bf),
            pltpu.VMEM((H * HB, width), bf),
            pltpu.VMEM((NZ - 1, HB, half), bf),
            pltpu.VMEM((HB, half), bf),
            pltpu.VMEM((3, HB, half), bf),
            pltpu.VMEM((H * HB, width), bf),
            pltpu.VMEM((rows, width), bf),
            pltpu.VMEM((rows, width), bf),
            pltpu.VMEM((rows, width), f32),
            pltpu.VMEM((1, rows), f32),
            pltpu.VMEM((7, 1, rows), f32),
            pltpu.VMEM((1, rows), f32),
            pltpu.VMEM((7, 1, rows), f32),
            pltpu.VMEM((1, rows), f32),
            pltpu.VMEM((7, 1, rows), f32),
            dma((6,)),
            dma((64,)),
            dma((NZ - 1,)),
            dma((3,)),
            dma((NZ - 1,)),
            dma((NZ - 1,)),
            dma((3,)),
            dma((NZ - 1,)),
            dma((2,)),
            dma((7,)),
            dma((7,)),
            dma((7,)),
        ],
        compiler_params=pltpu.CompilerParams(collective_id=0, has_side_effects=True),
        name="retriever",
    )(queries, passages, positive.reshape(1, rows), hard_owner, hard_block, hard_pick)
    return (loss[0, 0], grads[0], grads[1])


def solution(mesh):
    placed = (
        P(("blk", "neg"), None),
        P(("blk", "neg"), None),
        P(("blk", "neg")),
        P("blk", None),
        P("blk", None),
        P(("blk", "neg"), None),
    )
    return jax.shard_map(
        body,
        mesh=mesh,
        in_specs=placed,
        out_specs=(P(), P(("blk", "neg"), None), P(("blk", "neg"), None)),
        check_vma=False,
    )
```

```python
import functools

import jax
import jax.numpy as jnp
from jax import lax
from jax.experimental import pallas as pl
from jax.experimental.pallas import tpu as pltpu
from jax.sharding import PartitionSpec as P

MESH = pl.DeviceIdType.MESH
H = 4
HB = 16
GQ = 64
NZ = 8
NX = 4
NYL = 4
ZORDER = (4, 3, 5, 2, 6, 1, 7)


def nt(a, b):
    return lax.dot_general(a, b, (((1,), (1,)), ((), ())), preferred_element_type=jnp.float32)


def nn(a, b):
    return lax.dot_general(a, b, (((1,), (0,)), ((), ())), preferred_element_type=jnp.float32)


def tn(a, b):
    return lax.dot_general(a, b, (((0,), (0,)), ((), ())), preferred_element_type=jnp.float32)


def kernel(
    n_all,
    q_hbm, p_hbm, pos_hbm, own_hbm, blk_hbm, pick_hbm,
    loss_ref, out_ref,
    pos_ref, own_ref, blk_ref, pick_ref,
    qv, pv, cv, hv, fsend, frecv, fx, fxr,
    gsend, grecv, gx, gxr, gt, cgs, cgr, og,
    l1, l1r, l2, l2r, l3, l3r,
    lsem, ss, fr_s, fx_s, fa_s, gr_s, gx_s, ga_s, c_s, l1_s, l2_s, l3_s,
):
    blk = lax.axis_index("blk")
    neg = lax.axis_index("neg")
    rows, width = p_hbm.shape
    scale = width ** (-0.5)
    half = width // 2
    z = neg // 4
    yh = (neg // 2) % 2
    core = neg % 2
    x = blk // NYL
    yl = blk % NYL
    y = yh * NYL + yl

    zpeer = {d: {"blk": blk, "neg": ((z + d) % NZ) * 4 + yh * 2 + core} for d in range(1, NZ)}
    ypeer = {
        d: {
            "blk": x * NYL + ((y + d) % 8) % NYL,
            "neg": z * 4 + (((y + d) % 8) // NYL) * 2 + core,
        }
        for d in range(1, 8)
    }
    xpeer = {}
    for d in range(1, 8):
        xpeer[d] = {
            "blk": ((x + d // 2) % NX) * NYL + yl,
            "neg": z * 4 + yh * 2 + (core + d % 2) % 2,
        }
    mpeer = {
        d: {"blk": blk, "neg": z * 4 + ((yh + d // 2) % 2) * 2 + (core + d % 2) % 2}
        for d in range(1, 4)
    }
    after = {"blk": (blk + 1) % 16, "neg": neg}
    before = {"blk": (blk + 15) % 16, "neg": neg}

    load_p = pltpu.make_async_copy(p_hbm, pv, lsem.at[0])
    load_q = pltpu.make_async_copy(q_hbm, qv, lsem.at[1])
    load_own = pltpu.make_async_copy(own_hbm, own_ref, lsem.at[2])
    load_blk = pltpu.make_async_copy(blk_hbm, blk_ref, lsem.at[3])
    load_pos = pltpu.make_async_copy(pos_hbm, pos_ref, lsem.at[4])
    load_pick = pltpu.make_async_copy(pick_hbm, pick_ref, lsem.at[5])
    load_p.start()

    barrier = pltpu.get_barrier_semaphore()
    greet = [zpeer[4], mpeer[3], ypeer[4], after, before]
    greet += [zpeer[d] for d in ZORDER[1:]]
    greet += [ypeer[d] for d in ZORDER[1:]]
    greet += [xpeer[d] for d in (5, 4, 3, 2, 7, 6, 1)]
    for who in greet:
        pl.semaphore_signal(barrier, inc=1, device_id=who, device_id_type=MESH)
    load_own.start()
    load_blk.start()
    load_q.start()
    load_pos.start()
    load_pick.start()

    load_own.wait()
    load_blk.wait()
    srow = lax.broadcasted_iota(jnp.int32, (H * HB, rows), 0)
    owner = jnp.zeros_like(srow)
    place = jnp.zeros_like(srow)
    for h in range(H):
        owner = jnp.where(srow // HB == h, own_ref[:, h:h + 1], owner)
        place = jnp.where(srow // HB == h, blk_ref[:, h:h + 1], place)
    chosen = (owner == neg) & (place * HB + srow % HB == lax.broadcasted_iota(jnp.int32, srow.shape, 1))
    sel = chosen.astype(jnp.float32).astype(jnp.bfloat16)
    load_p.wait()
    fsend[...] = nn(sel, pv[...]).astype(jnp.bfloat16)
    pl.semaphore_wait(barrier, len(greet))

    sent = []

    def push(src, dst, send, recv, who):
        copy = pltpu.make_async_remote_copy(
            src_ref=src, dst_ref=dst, send_sem=send, recv_sem=recv,
            device_id=who, device_id_type=MESH,
        )
        copy.start()
        sent.append(copy)
        return copy

    def leave():
        for copy in sent:
            copy.wait_send()
        sent.clear()

    def part(ref, index):
        return ref.at[
            pl.ds(pl.multiple_of((index // 2) * HB, HB), HB),
            pl.ds(pl.multiple_of((index % 2) * half, half), half),
        ]

    sends = iter(range(64))

    def scatter(buf, land, sem):
        return [
            push(part(buf, (z + d) % NZ), land.at[d - 1], ss.at[next(sends)], sem.at[d - 1], zpeer[d])
            for d in ZORDER
        ]

    def gather(buf, sem):
        return [
            push(part(buf, z), part(buf, z), ss.at[next(sends)], sem.at[d - 1], zpeer[d])
            for d in ZORDER
        ]

    def middle(buf, land, sem):
        return [
            push(buf, land.at[d - 1], ss.at[next(sends)], sem.at[d - 1], mpeer[d]) for d in (3, 2, 1)
        ]

    def arrive(copies):
        for copy in copies:
            copy.wait_recv()

    def load_part(ref):
        return part(ref, z)[...].astype(jnp.float32)

    f1 = scatter(fsend, frecv, fr_s)
    cyc = push(pv, cv, ss.at[next(sends)], c_s.at[0], after)

    scol = lax.broadcasted_iota(jnp.int32, (rows, H * HB), 1)
    owner_t = jnp.zeros_like(scol)
    place_t = jnp.zeros_like(scol)
    for h in range(H):
        owner_t = jnp.where(scol // HB == h, own_ref[:, h:h + 1], owner_t)
        place_t = jnp.where(scol // HB == h, blk_ref[:, h:h + 1], place_t)
    chosen_t = (owner_t == neg) & (
        place_t * HB + scol % HB == lax.broadcasted_iota(jnp.int32, scol.shape, 0)
    )
    sel_t = chosen_t.astype(jnp.float32).astype(jnp.bfloat16)
    load_q.wait()
    load_pos.wait()
    load_pick.wait()
    q = qv[...]
    s0 = nt(pv[...], q) * scale
    hot = lax.broadcasted_iota(jnp.int32, s0.shape, 0) == pos_ref[...]
    spos = jnp.sum(jnp.where(hot, s0, 0.0), axis=0, keepdims=True)

    arrive(f1)
    fx[...] = (load_part(fsend) + jnp.sum(frecv[...].astype(jnp.float32), axis=0)).astype(jnp.bfloat16)
    f2 = middle(fx, fxr, fx_s)
    arrive(f2)
    part(hv, z)[...] = (
        fx[...].astype(jnp.float32) + jnp.sum(fxr[...].astype(jnp.float32), axis=0)
    ).astype(jnp.bfloat16)
    f3 = gather(hv, fa_s)
    cyc.wait_recv()
    s1 = nt(cv[...], q) * scale
    top01 = jnp.maximum(jnp.max(s0, axis=0, keepdims=True), jnp.max(s1, axis=0, keepdims=True))
    sum01 = jnp.sum(jnp.exp(s0 - top01), axis=0, keepdims=True) + jnp.sum(
        jnp.exp(s1 - top01), axis=0, keepdims=True
    )
    lane = lax.broadcasted_iota(jnp.int32, (H * HB, rows), 1)
    slot = lax.broadcasted_iota(jnp.int32, (H * HB, rows), 0) // HB
    first = jnp.where(lane < GQ, pick_ref[0:1, 0:1], pick_ref[1:2, 0:1])
    second = jnp.where(lane < GQ, pick_ref[0:1, 1:2], pick_ref[1:2, 1:2])
    picked = (slot == first) | (slot == second)
    arrive(f3)
    s2 = nt(hv[...], q) * scale

    s2 = jnp.where(picked, s2, -jnp.inf)
    top = jnp.maximum(top01, jnp.max(s2, axis=0, keepdims=True))
    total = sum01 * jnp.exp(top01 - top) + jnp.sum(jnp.exp(s2 - top), axis=0, keepdims=True)
    lse = top + jnp.log(total)

    forward = list(sent)
    sent.clear()
    g2 = jnp.exp(s2 - lse).astype(jnp.bfloat16)
    gsend[...] = (nn(g2, q) * scale).astype(jnp.bfloat16)
    b1 = scatter(gsend, grecv, gr_s)

    l1[...] = lse - spos
    a1 = [push(l1, l1r.at[d - 1], ss.at[next(sends)], l1_s.at[d - 1], zpeer[d]) for d in ZORDER]

    g1 = jnp.exp(s1 - lse).astype(jnp.bfloat16)
    cgs[...] = (nn(g1, q) * scale).astype(jnp.bfloat16)
    back = push(cgs, cgr, ss.at[next(sends)], c_s.at[1], before)

    g0 = (jnp.exp(s0 - lse) - hot.astype(jnp.float32)).astype(jnp.bfloat16)
    og[...] = nn(g0, q) * scale
    out_ref[0] = ((tn(g0, pv[...]) + tn(g1, cv[...]) + tn(g2, hv[...])) * scale).astype(jnp.bfloat16)

    for copy in forward:
        copy.wait_send()
    arrive(b1)
    gx[...] = (load_part(gsend) + jnp.sum(grecv[...].astype(jnp.float32), axis=0)).astype(jnp.bfloat16)
    b2 = middle(gx, gxr, gx_s)
    arrive(a1)
    l2[...] = l1[...] + jnp.sum(l1r[...], axis=0)
    a2 = [push(l2, l2r.at[d - 1], ss.at[next(sends)], l2_s.at[d - 1], ypeer[d]) for d in ZORDER]
    arrive(b2)
    part(gt, z)[...] = (
        gx[...].astype(jnp.float32) + jnp.sum(gxr[...].astype(jnp.float32), axis=0)
    ).astype(jnp.bfloat16)
    b3 = gather(gt, ga_s)
    arrive(a2)
    l3[...] = l2[...] + jnp.sum(l2r[...], axis=0)
    a3 = [push(l3, l3r.at[d - 1], ss.at[next(sends)], l3_s.at[d - 1], xpeer[d]) for d in range(1, 8)]
    back.wait_recv()
    og[...] += cgr[...].astype(jnp.float32)
    arrive(a3)
    loss_ref[0, 0] = jnp.sum(l3[...] + jnp.sum(l3r[...], axis=0)) / n_all
    leave()
    arrive(b3)
    out_ref[1] = (og[...] + nn(sel_t, gt[...])).astype(jnp.bfloat16)


def body(queries, passages, positive, hard_owner, hard_block, hard_pick):
    rows, width = passages.shape
    n_all = rows * lax.axis_size("blk") * lax.axis_size("neg")
    bf = jnp.bfloat16
    f32 = jnp.float32
    any_space = pl.BlockSpec(memory_space=pl.ANY)
    vmem = pl.BlockSpec(memory_space=pltpu.VMEM)
    smem = pl.BlockSpec(memory_space=pltpu.SMEM)
    half = width // 2
    dma = pltpu.SemaphoreType.DMA
    loss, grads = pl.pallas_call(
        functools.partial(kernel, n_all),
        out_shape=(
            pltpu.SMEM((1, 1), f32),
            pltpu.VMEM((2, rows, width), bf),
        ),
        in_specs=[any_space] * 6,
        out_specs=(smem, vmem),
        scratch_shapes=[
            pltpu.VMEM((1, rows), jnp.int32),
            pltpu.VMEM(hard_owner.shape, jnp.int32),
            pltpu.VMEM(hard_block.shape, jnp.int32),
            pltpu.VMEM(hard_pick.shape, jnp.int32),
            pltpu.VMEM((rows, width), bf),
            pltpu.VMEM((rows, width), bf),
            pltpu.VMEM((rows, width), bf),
            pltpu.VMEM((H * HB, width), bf),
            pltpu.VMEM((H * HB, width), bf),
            pltpu.VMEM((NZ - 1, HB, half), bf),
            pltpu.VMEM((HB, half), bf),
            pltpu.VMEM((3, HB, half), bf),
            pltpu.VMEM((H * HB, width), bf),
            pltpu.VMEM((NZ - 1, HB, half), bf),
            pltpu.VMEM((HB, half), bf),
            pltpu.VMEM((3, HB, half), bf),
            pltpu.VMEM((H * HB, width), bf),
            pltpu.VMEM((rows, width), bf),
            pltpu.VMEM((rows, width), bf),
            pltpu.VMEM((rows, width), f32),
            pltpu.VMEM((1, rows), f32),
            pltpu.VMEM((7, 1, rows), f32),
            pltpu.VMEM((1, rows), f32),
            pltpu.VMEM((7, 1, rows), f32),
            pltpu.VMEM((1, rows), f32),
            pltpu.VMEM((7, 1, rows), f32),
            dma((6,)),
            dma((64,)),
            dma((NZ - 1,)),
            dma((3,)),
            dma((NZ - 1,)),
            dma((NZ - 1,)),
            dma((3,)),
            dma((NZ - 1,)),
            dma((2,)),
            dma((7,)),
            dma((7,)),
            dma((7,)),
        ],
        compiler_params=pltpu.CompilerParams(collective_id=0, has_side_effects=True),
        name="retriever",
    )(queries, passages, positive.reshape(1, rows), hard_owner, hard_block, hard_pick)
    return (loss[0, 0], grads[0], grads[1])


def solution(mesh):
    placed = (
        P(("blk", "neg"), None),
        P(("blk", "neg"), None),
        P(("blk", "neg")),
        P("blk", None),
        P("blk", None),
        P(("blk", "neg"), None),
    )
    return jax.shard_map(
        body,
        mesh=mesh,
        in_specs=placed,
        out_specs=(P(), P(("blk", "neg"), None), P(("blk", "neg"), None)),
        check_vma=False,
    )
```

```python
import functools

import jax
import jax.numpy as jnp
from jax import lax
from jax.experimental import pallas as pl
from jax.experimental.pallas import tpu as pltpu
from jax.sharding import PartitionSpec as P

MESH = pl.DeviceIdType.MESH
H = 4
HB = 16
GQ = 64
NZ = 8
NX = 4
NYL = 4
ZORDER = (4, 3, 5, 2, 6, 1, 7)


def nt(a, b):
    return lax.dot_general(a, b, (((1,), (1,)), ((), ())), preferred_element_type=jnp.float32)


def nn(a, b):
    return lax.dot_general(a, b, (((1,), (0,)), ((), ())), preferred_element_type=jnp.float32)


def tn(a, b):
    return lax.dot_general(a, b, (((0,), (0,)), ((), ())), preferred_element_type=jnp.float32)


def kernel(
    n_all,
    q_hbm, p_hbm, pos_hbm, own_hbm, blk_hbm, pick_hbm,
    loss_ref, out_ref,
    pos_ref, own_ref, blk_ref, pick_ref,
    qv, pv, cv, hv, fsend, frecv, fx, fxr,
    gsend, grecv, gx, gxr, gt, cgs, cgr, og,
    l1, l1r, l2, l2r, l3, l3r,
    lsem, fr_s, fx_s, fa_s, gr_s, gx_s, ga_s, c_s, k_s, l1_s, l2_s, l3_s,
):
    blk = lax.axis_index("blk")
    neg = lax.axis_index("neg")
    rows, width = p_hbm.shape
    scale = width ** (-0.5)
    half = width // 2
    z = neg // 4
    yh = (neg // 2) % 2
    core = neg % 2
    x = blk // NYL
    yl = blk % NYL
    y = yh * NYL + yl

    zpeer = {d: {"blk": blk, "neg": ((z + d) % NZ) * 4 + yh * 2 + core} for d in range(1, NZ)}
    ypeer = {
        d: {
            "blk": x * NYL + ((y + d) % 8) % NYL,
            "neg": z * 4 + (((y + d) % 8) // NYL) * 2 + core,
        }
        for d in range(1, 8)
    }
    xpeer = {}
    for d in range(1, 8):
        xpeer[d] = {
            "blk": ((x + d // 2) % NX) * NYL + yl,
            "neg": z * 4 + yh * 2 + (core + d % 2) % 2,
        }
    mpeer = {
        d: {"blk": blk, "neg": z * 4 + ((yh + d // 2) % 2) * 2 + (core + d % 2) % 2}
        for d in range(1, 4)
    }
    after = {"blk": (blk + 1) % 16, "neg": neg}
    before = {"blk": (blk + 15) % 16, "neg": neg}

    load_p = pltpu.make_async_copy(p_hbm, pv, lsem.at[0])
    load_q = pltpu.make_async_copy(q_hbm, qv, lsem.at[1])
    load_own = pltpu.make_async_copy(own_hbm, own_ref, lsem.at[2])
    load_blk = pltpu.make_async_copy(blk_hbm, blk_ref, lsem.at[3])
    load_pos = pltpu.make_async_copy(pos_hbm, pos_ref, lsem.at[4])
    load_pick = pltpu.make_async_copy(pick_hbm, pick_ref, lsem.at[5])
    load_p.start()

    barrier = pltpu.get_barrier_semaphore()
    greet = [zpeer[4], mpeer[3], ypeer[4], after, before]
    greet += [zpeer[d] for d in ZORDER[1:]]
    greet += [ypeer[d] for d in ZORDER[1:]]
    greet += [xpeer[d] for d in (5, 4, 3, 2, 7, 6, 1)]
    for who in greet:
        pl.semaphore_signal(barrier, inc=1, device_id=who, device_id_type=MESH)
    load_own.start()
    load_blk.start()
    load_q.start()
    load_pos.start()
    load_pick.start()

    load_own.wait()
    load_blk.wait()
    srow = lax.broadcasted_iota(jnp.int32, (H * HB, rows), 0)
    owner = jnp.zeros_like(srow)
    place = jnp.zeros_like(srow)
    for h in range(H):
        owner = jnp.where(srow // HB == h, own_ref[:, h:h + 1], owner)
        place = jnp.where(srow // HB == h, blk_ref[:, h:h + 1], place)
    chosen = (owner == neg) & (place * HB + srow % HB == lax.broadcasted_iota(jnp.int32, srow.shape, 1))
    sel = chosen.astype(jnp.float32).astype(jnp.bfloat16)
    load_p.wait()
    fsend[...] = nn(sel, pv[...]).astype(jnp.bfloat16)
    pl.semaphore_wait(barrier, len(greet))

    def push(src, dst, sems, who):
        pltpu.make_async_remote_copy(
            src_ref=src, dst_ref=dst, send_sem=sems.at[0], recv_sem=sems.at[1],
            device_id=who, device_id_type=MESH,
        ).start()

    def all_of(ref, sems):
        return pltpu.make_async_remote_copy(
            src_ref=ref, dst_ref=ref, send_sem=sems.at[0], recv_sem=sems.at[1],
            device_id=after, device_id_type=MESH,
        )

    def arrive(ref, sems):
        all_of(ref, sems).wait_recv()

    def leave(ref, sems):
        all_of(ref, sems).wait_send()

    def part(ref, index):
        return ref.at[
            pl.ds(pl.multiple_of((index // 2) * HB, HB), HB),
            pl.ds(pl.multiple_of((index % 2) * half, half), half),
        ]

    def scatter(buf, land, sems):
        for d in ZORDER:
            push(part(buf, (z + d) % NZ), land.at[d - 1], sems, zpeer[d])

    def gather(buf, sems):
        for d in ZORDER:
            push(part(buf, z), part(buf, z), sems, zpeer[d])

    def middle(buf, land, sems):
        for d in (3, 2, 1):
            push(buf, land.at[d - 1], sems, mpeer[d])

    def load_part(ref):
        return part(ref, z)[...].astype(jnp.float32)

    scatter(fsend, frecv, fr_s)
    push(pv, cv, c_s, after)

    scol = lax.broadcasted_iota(jnp.int32, (rows, H * HB), 1)
    owner_t = jnp.zeros_like(scol)
    place_t = jnp.zeros_like(scol)
    for h in range(H):
        owner_t = jnp.where(scol // HB == h, own_ref[:, h:h + 1], owner_t)
        place_t = jnp.where(scol // HB == h, blk_ref[:, h:h + 1], place_t)
    chosen_t = (owner_t == neg) & (
        place_t * HB + scol % HB == lax.broadcasted_iota(jnp.int32, scol.shape, 0)
    )
    sel_t = chosen_t.astype(jnp.float32).astype(jnp.bfloat16)
    load_q.wait()
    load_pos.wait()
    load_pick.wait()
    q = qv[...]
    s0 = nt(pv[...], q) * scale
    hot = lax.broadcasted_iota(jnp.int32, s0.shape, 0) == pos_ref[...]
    spos = jnp.sum(jnp.where(hot, s0, 0.0), axis=0, keepdims=True)

    arrive(frecv, fr_s)
    fx[...] = (load_part(fsend) + jnp.sum(frecv[...].astype(jnp.float32), axis=0)).astype(jnp.bfloat16)
    middle(fx, fxr, fx_s)
    arrive(fxr, fx_s)
    part(hv, z)[...] = (
        fx[...].astype(jnp.float32) + jnp.sum(fxr[...].astype(jnp.float32), axis=0)
    ).astype(jnp.bfloat16)
    gather(hv, fa_s)
    arrive(cv, c_s)
    s1 = nt(cv[...], q) * scale
    top01 = jnp.maximum(jnp.max(s0, axis=0, keepdims=True), jnp.max(s1, axis=0, keepdims=True))
    sum01 = jnp.sum(jnp.exp(s0 - top01), axis=0, keepdims=True) + jnp.sum(
        jnp.exp(s1 - top01), axis=0, keepdims=True
    )
    lane = lax.broadcasted_iota(jnp.int32, (H * HB, rows), 1)
    slot = lax.broadcasted_iota(jnp.int32, (H * HB, rows), 0) // HB
    first = jnp.where(lane < GQ, pick_ref[0:1, 0:1], pick_ref[1:2, 0:1])
    second = jnp.where(lane < GQ, pick_ref[0:1, 1:2], pick_ref[1:2, 1:2])
    picked = (slot == first) | (slot == second)
    arrive(frecv, fa_s)
    s2 = nt(hv[...], q) * scale

    s2 = jnp.where(picked, s2, -jnp.inf)
    top = jnp.maximum(top01, jnp.max(s2, axis=0, keepdims=True))
    total = sum01 * jnp.exp(top01 - top) + jnp.sum(jnp.exp(s2 - top), axis=0, keepdims=True)
    lse = top + jnp.log(total)

    g2 = jnp.exp(s2 - lse).astype(jnp.bfloat16)
    gsend[...] = (nn(g2, q) * scale).astype(jnp.bfloat16)
    scatter(gsend, grecv, gr_s)

    l1[...] = lse - spos
    for d in ZORDER:
        push(l1, l1r.at[d - 1], l1_s, zpeer[d])

    g1 = jnp.exp(s1 - lse).astype(jnp.bfloat16)
    cgs[...] = (nn(g1, q) * scale).astype(jnp.bfloat16)
    push(cgs, cgr, k_s, before)

    g0 = (jnp.exp(s0 - lse) - hot.astype(jnp.float32)).astype(jnp.bfloat16)
    og[...] = nn(g0, q) * scale
    out_ref[0] = ((tn(g0, pv[...]) + tn(g1, cv[...]) + tn(g2, hv[...])) * scale).astype(jnp.bfloat16)

    leave(frecv, fr_s)
    leave(fxr, fx_s)
    leave(frecv, fa_s)
    leave(cv, c_s)
    arrive(grecv, gr_s)
    gx[...] = (load_part(gsend) + jnp.sum(grecv[...].astype(jnp.float32), axis=0)).astype(jnp.bfloat16)
    middle(gx, gxr, gx_s)
    arrive(l1r, l1_s)
    l2[...] = l1[...] + jnp.sum(l1r[...], axis=0)
    for d in ZORDER:
        push(l2, l2r.at[d - 1], l2_s, ypeer[d])
    arrive(gxr, gx_s)
    part(gt, z)[...] = (
        gx[...].astype(jnp.float32) + jnp.sum(gxr[...].astype(jnp.float32), axis=0)
    ).astype(jnp.bfloat16)
    gather(gt, ga_s)
    arrive(l2r, l2_s)
    l3[...] = l2[...] + jnp.sum(l2r[...], axis=0)
    for d in range(1, 8):
        push(l3, l3r.at[d - 1], l3_s, xpeer[d])
    arrive(cgr, k_s)
    og[...] += cgr[...].astype(jnp.float32)
    arrive(l3r, l3_s)
    loss_ref[0, 0] = jnp.sum(l3[...] + jnp.sum(l3r[...], axis=0)) / n_all
    leave(grecv, gr_s)
    leave(gxr, gx_s)
    leave(grecv, ga_s)
    leave(cgr, k_s)
    leave(l1r, l1_s)
    leave(l2r, l2_s)
    leave(l3r, l3_s)
    arrive(grecv, ga_s)
    out_ref[1] = (og[...] + nn(sel_t, gt[...])).astype(jnp.bfloat16)


def body(queries, passages, positive, hard_owner, hard_block, hard_pick):
    rows, width = passages.shape
    n_all = rows * lax.axis_size("blk") * lax.axis_size("neg")
    bf = jnp.bfloat16
    f32 = jnp.float32
    any_space = pl.BlockSpec(memory_space=pl.ANY)
    vmem = pl.BlockSpec(memory_space=pltpu.VMEM)
    smem = pl.BlockSpec(memory_space=pltpu.SMEM)
    half = width // 2
    dma = pltpu.SemaphoreType.DMA
    loss, grads = pl.pallas_call(
        functools.partial(kernel, n_all),
        out_shape=(
            pltpu.SMEM((1, 1), f32),
            pltpu.VMEM((2, rows, width), bf),
        ),
        in_specs=[any_space] * 6,
        out_specs=(smem, vmem),
        scratch_shapes=[
            pltpu.VMEM((1, rows), jnp.int32),
            pltpu.VMEM(hard_owner.shape, jnp.int32),
            pltpu.VMEM(hard_block.shape, jnp.int32),
            pltpu.VMEM(hard_pick.shape, jnp.int32),
            pltpu.VMEM((rows, width), bf),
            pltpu.VMEM((rows, width), bf),
            pltpu.VMEM((rows, width), bf),
            pltpu.VMEM((H * HB, width), bf),
            pltpu.VMEM((H * HB, width), bf),
            pltpu.VMEM((NZ - 1, HB, half), bf),
            pltpu.VMEM((HB, half), bf),
            pltpu.VMEM((3, HB, half), bf),
            pltpu.VMEM((H * HB, width), bf),
            pltpu.VMEM((NZ - 1, HB, half), bf),
            pltpu.VMEM((HB, half), bf),
            pltpu.VMEM((3, HB, half), bf),
            pltpu.VMEM((H * HB, width), bf),
            pltpu.VMEM((rows, width), bf),
            pltpu.VMEM((rows, width), bf),
            pltpu.VMEM((rows, width), f32),
            pltpu.VMEM((1, rows), f32),
            pltpu.VMEM((7, 1, rows), f32),
            pltpu.VMEM((1, rows), f32),
            pltpu.VMEM((7, 1, rows), f32),
            pltpu.VMEM((1, rows), f32),
            pltpu.VMEM((7, 1, rows), f32),
            dma((6,)),
            dma((2,)),
            dma((2,)),
            dma((2,)),
            dma((2,)),
            dma((2,)),
            dma((2,)),
            dma((2,)),
            dma((2,)),
            dma((2,)),
            dma((2,)),
            dma((2,)),
        ],
        compiler_params=pltpu.CompilerParams(collective_id=0, has_side_effects=True),
        name="retriever",
    )(queries, passages, positive.reshape(1, rows), hard_owner, hard_block, hard_pick)
    return (loss[0, 0], grads[0], grads[1])


def solution(mesh):
    placed = (
        P(("blk", "neg"), None),
        P(("blk", "neg"), None),
        P(("blk", "neg")),
        P("blk", None),
        P("blk", None),
        P(("blk", "neg"), None),
    )
    return jax.shard_map(
        body,
        mesh=mesh,
        in_specs=placed,
        out_specs=(P(), P(("blk", "neg"), None), P(("blk", "neg"), None)),
        check_vma=False,
    )
```

```python
import functools

import jax
import jax.numpy as jnp
from jax import lax
from jax.experimental import pallas as pl
from jax.experimental.pallas import tpu as pltpu
from jax.sharding import PartitionSpec as P

MESH = pl.DeviceIdType.MESH
H = 4
HB = 16
GQ = 64
SHARED = H * HB
NZ = 8
NX = 4
NYL = 4
ZORDER = (4, 3, 5, 2, 6, 1, 7)


def nn(a, b):
    return lax.dot_general(a, b, (((1,), (0,)), ((), ())), preferred_element_type=jnp.float32)


def tn(a, b):
    return lax.dot_general(a, b, (((0,), (0,)), ((), ())), preferred_element_type=jnp.float32)


def kernel(
    n_all,
    q_hbm, p_hbm, pos_hbm, own_hbm, blk_hbm, pick_hbm,
    loss_ref, out_ref,
    pos_ref, own_ref, blk_ref, pick_ref,
    qt, qv, pv, cv, hv, fsend, frecv, fx, fxr,
    gsend, grecv, gx, gxr, gt, cgs, cgr, og,
    l1, l1r, l2, l2r, l3, l3r,
    lsem, fr_s, fx_s, fa_s, gr_s, gx_s, ga_s, c_s, k_s, l1_s, l2_s, l3_s,
):
    blk = lax.axis_index("blk")
    neg = lax.axis_index("neg")
    rows, width = p_hbm.shape
    scale = width ** (-0.5)
    half = width // 2
    z = lax.div(neg, 4)
    yc = lax.rem(neg, 4)
    yh = lax.div(yc, 2)
    core = lax.rem(yc, 2)
    x = lax.div(blk, NYL)
    yl = lax.rem(blk, NYL)
    y = yh * NYL + yl
    zbase = z * 4

    zat = {d: lax.rem(z + d, NZ) for d in range(1, NZ)}
    zpeer = {d: {"blk": blk, "neg": zat[d] * 4 + yc} for d in range(1, NZ)}
    mpeer = {
        1: {"blk": blk, "neg": zbase + yh * 2 + (1 - core)},
        2: {"blk": blk, "neg": zbase + (1 - yh) * 2 + core},
        3: {"blk": blk, "neg": zbase + (1 - yh) * 2 + (1 - core)},
    }
    after = {"blk": lax.rem(blk + 1, 16), "neg": neg}
    before = {"blk": lax.rem(blk + 15, 16), "neg": neg}
    ypeer = {}
    for d in range(1, 8):
        yd = lax.rem(y + d, 8)
        ypeer[d] = {"blk": x * NYL + lax.rem(yd, NYL), "neg": zbase + lax.div(yd, NYL) * 2 + core}
    xpeer = {}
    for d in range(1, 8):
        xd = lax.rem(x + d // 2, NX)
        xpeer[d] = {"blk": xd * NYL + yl, "neg": mpeer[1]["neg"] if d % 2 else neg}

    load_p = pltpu.make_async_copy(p_hbm, pv, lsem.at[0])
    load_q = pltpu.make_async_copy(q_hbm, qv, lsem.at[1])
    load_own = pltpu.make_async_copy(own_hbm, own_ref, lsem.at[2])
    load_blk = pltpu.make_async_copy(blk_hbm, blk_ref, lsem.at[3])
    load_pos = pltpu.make_async_copy(pos_hbm, pos_ref, lsem.at[4])
    load_pick = pltpu.make_async_copy(pick_hbm, pick_ref, lsem.at[5])
    load_p.start()

    barrier = pltpu.get_barrier_semaphore()
    greet = [zpeer[4], mpeer[3], ypeer[4], after, before]
    greet += [zpeer[d] for d in ZORDER[1:]]
    greet += [ypeer[d] for d in ZORDER[1:]]
    greet += [xpeer[d] for d in (5, 4, 3, 2, 7, 6, 1)]
    for who in greet:
        pl.semaphore_signal(barrier, inc=1, device_id=who, device_id_type=MESH)
    load_own.start()
    load_blk.start()
    load_q.start()
    load_pos.start()
    load_pick.start()

    load_own.wait()
    load_blk.wait()
    srow = lax.broadcasted_iota(jnp.int32, (H * HB, rows), 0)
    owner = jnp.zeros_like(srow)
    place = jnp.zeros_like(srow)
    for h in range(H):
        owner = jnp.where(srow // HB == h, own_ref[:, h:h + 1], owner)
        place = jnp.where(srow // HB == h, blk_ref[:, h:h + 1], place)
    chosen = (owner == neg) & (place * HB + srow % HB == lax.broadcasted_iota(jnp.int32, srow.shape, 1))
    sel = chosen.astype(jnp.float32).astype(jnp.bfloat16)
    load_p.wait()
    fsend[0:SHARED, :] = nn(sel, pv[:, :half]).astype(jnp.bfloat16)
    fsend[SHARED:, :] = nn(sel, pv[:, half:]).astype(jnp.bfloat16)
    pl.semaphore_wait(barrier, len(greet))

    def push(src, dst, sems, who):
        pltpu.make_async_remote_copy(
            src_ref=src, dst_ref=dst, send_sem=sems.at[0], recv_sem=sems.at[1],
            device_id=who, device_id_type=MESH,
        ).start()

    def all_of(ref, sems):
        return pltpu.make_async_remote_copy(
            src_ref=ref, dst_ref=ref, send_sem=sems.at[0], recv_sem=sems.at[1],
            device_id=after, device_id_type=MESH,
        )

    def arrive(ref, sems):
        all_of(ref, sems).wait_recv()

    def leave(ref, sems):
        all_of(ref, sems).wait_send()

    def part(ref, index):
        return ref.at[pl.ds(pl.multiple_of(index * HB, HB), HB), :]

    def scatter(buf, land, sems):
        for d in ZORDER:
            push(part(buf, zat[d]), land.at[d - 1], sems, zpeer[d])

    def gather(buf, sems):
        for d in ZORDER:
            push(part(buf, z), part(buf, z), sems, zpeer[d])

    def middle(buf, land, sems):
        for d in (3, 2, 1):
            push(buf, land.at[d - 1], sems, mpeer[d])

    def load_part(ref):
        return part(ref, z)[...].astype(jnp.float32)

    scatter(fsend, frecv, fr_s)
    push(pv, cv, c_s, after)

    scol = lax.broadcasted_iota(jnp.int32, (rows, H * HB), 1)
    owner_t = jnp.zeros_like(scol)
    place_t = jnp.zeros_like(scol)
    for h in range(H):
        owner_t = jnp.where(scol // HB == h, own_ref[:, h:h + 1], owner_t)
        place_t = jnp.where(scol // HB == h, blk_ref[:, h:h + 1], place_t)
    chosen_t = (owner_t == neg) & (
        place_t * HB + scol % HB == lax.broadcasted_iota(jnp.int32, scol.shape, 0)
    )
    sel_t = chosen_t.astype(jnp.float32).astype(jnp.bfloat16)
    load_q.wait()
    load_pos.wait()
    load_pick.wait()
    q = qv[...]
    qt[...] = q.T
    s0 = nn(pv[...], qt[...]) * scale
    hot = lax.broadcasted_iota(jnp.int32, s0.shape, 0) == pos_ref[...]
    spos = jnp.sum(jnp.where(hot, s0, 0.0), axis=0, keepdims=True)

    arrive(frecv, fr_s)
    fx[...] = (load_part(fsend) + jnp.sum(frecv[...].astype(jnp.float32), axis=0)).astype(jnp.bfloat16)
    middle(fx, fxr, fx_s)
    arrive(fxr, fx_s)
    part(hv, z)[...] = (
        fx[...].astype(jnp.float32) + jnp.sum(fxr[...].astype(jnp.float32), axis=0)
    ).astype(jnp.bfloat16)
    gather(hv, fa_s)
    arrive(cv, c_s)
    s1 = nn(cv[...], qt[...]) * scale
    top01 = jnp.maximum(jnp.max(s0, axis=0, keepdims=True), jnp.max(s1, axis=0, keepdims=True))
    sum01 = jnp.sum(jnp.exp(s0 - top01), axis=0, keepdims=True) + jnp.sum(
        jnp.exp(s1 - top01), axis=0, keepdims=True
    )
    lane = lax.broadcasted_iota(jnp.int32, (H * HB, rows), 1)
    slot = lax.broadcasted_iota(jnp.int32, (H * HB, rows), 0) // HB
    first = jnp.where(lane < GQ, pick_ref[0:1, 0:1], pick_ref[1:2, 0:1])
    second = jnp.where(lane < GQ, pick_ref[0:1, 1:2], pick_ref[1:2, 1:2])
    picked = (slot == first) | (slot == second)
    arrive(frecv, fa_s)
    s2 = (nn(hv[0:SHARED, :], qt[:half, :]) + nn(hv[SHARED:, :], qt[half:, :])) * scale

    s2 = jnp.where(picked, s2, -jnp.inf)
    top = jnp.maximum(top01, jnp.max(s2, axis=0, keepdims=True))
    total = sum01 * jnp.exp(top01 - top) + jnp.sum(jnp.exp(s2 - top), axis=0, keepdims=True)
    lse = top + jnp.log(total)

    g2 = jnp.exp(s2 - lse).astype(jnp.bfloat16)
    gsend[0:SHARED, :] = (nn(g2, q[:, :half]) * scale).astype(jnp.bfloat16)
    gsend[SHARED:, :] = (nn(g2, q[:, half:]) * scale).astype(jnp.bfloat16)
    scatter(gsend, grecv, gr_s)

    l1[...] = lse - spos
    for d in ZORDER:
        push(l1, l1r.at[d - 1], l1_s, zpeer[d])

    g1 = jnp.exp(s1 - lse).astype(jnp.bfloat16)
    cgs[...] = (nn(g1, q) * scale).astype(jnp.bfloat16)
    push(cgs, cgr, k_s, before)

    g0 = (jnp.exp(s0 - lse) - hot.astype(jnp.float32)).astype(jnp.bfloat16)
    og[...] = nn(g0, q) * scale
    for side, lo in ((0, 0), (1, half)):
        out_ref[0, :, lo:lo + half] = (
            (
                tn(g0, pv[:, lo:lo + half])
                + tn(g1, cv[:, lo:lo + half])
                + tn(g2, hv[side * SHARED:(side + 1) * SHARED, :])
            )
            * scale
        ).astype(jnp.bfloat16)

    leave(frecv, fr_s)
    leave(fxr, fx_s)
    leave(frecv, fa_s)
    leave(cv, c_s)
    arrive(grecv, gr_s)
    gx[...] = (load_part(gsend) + jnp.sum(grecv[...].astype(jnp.float32), axis=0)).astype(jnp.bfloat16)
    middle(gx, gxr, gx_s)
    arrive(l1r, l1_s)
    l2[...] = l1[...] + jnp.sum(l1r[...], axis=0)
    for d in ZORDER:
        push(l2, l2r.at[d - 1], l2_s, ypeer[d])
    arrive(gxr, gx_s)
    part(gt, z)[...] = (
        gx[...].astype(jnp.float32) + jnp.sum(gxr[...].astype(jnp.float32), axis=0)
    ).astype(jnp.bfloat16)
    gather(gt, ga_s)
    arrive(l2r, l2_s)
    l3[...] = l2[...] + jnp.sum(l2r[...], axis=0)
    for d in range(1, 8):
        push(l3, l3r.at[d - 1], l3_s, xpeer[d])
    arrive(cgr, k_s)
    og[...] += cgr[...].astype(jnp.float32)
    arrive(l3r, l3_s)
    loss_ref[0, 0] = jnp.sum(l3[...] + jnp.sum(l3r[...], axis=0)) / n_all
    leave(grecv, gr_s)
    leave(gxr, gx_s)
    leave(grecv, ga_s)
    leave(cgr, k_s)
    leave(l1r, l1_s)
    leave(l2r, l2_s)
    leave(l3r, l3_s)
    arrive(grecv, ga_s)
    for side, lo in ((0, 0), (1, half)):
        shared = gt[side * SHARED:(side + 1) * SHARED, :]
        out_ref[1, :, lo:lo + half] = (og[:, lo:lo + half] + nn(sel_t, shared)).astype(jnp.bfloat16)


def body(queries, passages, positive, hard_owner, hard_block, hard_pick):
    rows, width = passages.shape
    n_all = rows * lax.axis_size("blk") * lax.axis_size("neg")
    bf = jnp.bfloat16
    f32 = jnp.float32
    any_space = pl.BlockSpec(memory_space=pl.ANY)
    vmem = pl.BlockSpec(memory_space=pltpu.VMEM)
    smem = pl.BlockSpec(memory_space=pltpu.SMEM)
    half = width // 2
    dma = pltpu.SemaphoreType.DMA
    loss, grads = pl.pallas_call(
        functools.partial(kernel, n_all),
        out_shape=(
            pltpu.SMEM((1, 1), f32),
            pltpu.VMEM((2, rows, width), bf),
        ),
        in_specs=[any_space] * 6,
        out_specs=(smem, vmem),
        scratch_shapes=[
            pltpu.VMEM((1, rows), jnp.int32),
            pltpu.VMEM(hard_owner.shape, jnp.int32),
            pltpu.VMEM(hard_block.shape, jnp.int32),
            pltpu.VMEM(hard_pick.shape, jnp.int32),
            pltpu.VMEM((width, rows), bf),
            pltpu.VMEM((rows, width), bf),
            pltpu.VMEM((rows, width), bf),
            pltpu.VMEM((rows, width), bf),
            pltpu.VMEM((2 * SHARED, half), bf),
            pltpu.VMEM((2 * SHARED, half), bf),
            pltpu.VMEM((NZ - 1, HB, half), bf),
            pltpu.VMEM((HB, half), bf),
            pltpu.VMEM((3, HB, half), bf),
            pltpu.VMEM((2 * SHARED, half), bf),
            pltpu.VMEM((NZ - 1, HB, half), bf),
            pltpu.VMEM((HB, half), bf),
            pltpu.VMEM((3, HB, half), bf),
            pltpu.VMEM((2 * SHARED, half), bf),
            pltpu.VMEM((rows, width), bf),
            pltpu.VMEM((rows, width), bf),
            pltpu.VMEM((rows, width), f32),
            pltpu.VMEM((1, rows), f32),
            pltpu.VMEM((7, 1, rows), f32),
            pltpu.VMEM((1, rows), f32),
            pltpu.VMEM((7, 1, rows), f32),
            pltpu.VMEM((1, rows), f32),
            pltpu.VMEM((7, 1, rows), f32),
            dma((6,)),
            dma((2,)),
            dma((2,)),
            dma((2,)),
            dma((2,)),
            dma((2,)),
            dma((2,)),
            dma((2,)),
            dma((2,)),
            dma((2,)),
            dma((2,)),
            dma((2,)),
        ],
        compiler_params=pltpu.CompilerParams(collective_id=0, has_side_effects=True),
        name="retriever",
    )(queries, passages, positive.reshape(1, rows), hard_owner, hard_block, hard_pick)
    return (loss[0, 0], grads[0], grads[1])


def solution(mesh):
    placed = (
        P(("blk", "neg"), None),
        P(("blk", "neg"), None),
        P(("blk", "neg")),
        P("blk", None),
        P("blk", None),
        P(("blk", "neg"), None),
    )
    return jax.shard_map(
        body,
        mesh=mesh,
        in_specs=placed,
        out_specs=(P(), P(("blk", "neg"), None), P(("blk", "neg"), None)),
        check_vma=False,
    )
```

```python
import functools

import jax
import jax.numpy as jnp
from jax import lax
from jax.experimental import pallas as pl
from jax.experimental.pallas import tpu as pltpu
from jax.sharding import PartitionSpec as P

MESH = pl.DeviceIdType.MESH
H = 4
HB = 16
GQ = 64
SHARED = H * HB
NZ = 8
NX = 4
NYL = 4
ZORDER = (4, 3, 5, 2, 6, 1, 7)


def nn(a, b):
    return lax.dot_general(a, b, (((1,), (0,)), ((), ())), preferred_element_type=jnp.float32)


def tn(a, b):
    return lax.dot_general(a, b, (((0,), (0,)), ((), ())), preferred_element_type=jnp.float32)


def kernel(
    n_all,
    q_hbm, p_hbm, pos_hbm, own_hbm, blk_hbm, pick_hbm,
    loss_ref, out_ref,
    pos_ref, own_ref, blk_ref, pick_ref,
    qt, qv, pv, cv, hv, fsend, frecv, fx, fxr,
    gsend, grecv, gx, gxr, gt, cgs, cgr, og,
    l1, l1r, l2, l2r, l3, l3r,
    lsem, fr_s, fx_s, fa_s, gr_s, gx_s, ga_s, c_s, k_s, l1_s, l2_s, l3_s,
):
    blk = lax.axis_index("blk")
    neg = lax.axis_index("neg")
    rows, width = p_hbm.shape
    scale = width ** (-0.5)
    half = width // 2
    z = lax.div(neg, 4)
    yc = lax.rem(neg, 4)
    yh = lax.div(yc, 2)
    core = lax.rem(yc, 2)
    x = lax.div(blk, NYL)
    yl = lax.rem(blk, NYL)
    y = yh * NYL + yl
    zbase = z * 4

    zat = {d: lax.rem(z + d, NZ) for d in range(1, NZ)}
    zpeer = {d: {"blk": blk, "neg": zat[d] * 4 + yc} for d in range(1, NZ)}
    mpeer = {
        1: {"blk": blk, "neg": zbase + yh * 2 + (1 - core)},
        2: {"blk": blk, "neg": zbase + (1 - yh) * 2 + core},
        3: {"blk": blk, "neg": zbase + (1 - yh) * 2 + (1 - core)},
    }
    after = {"blk": lax.rem(blk + 1, 16), "neg": neg}
    before = {"blk": lax.rem(blk + 15, 16), "neg": neg}
    ypeer = {}
    for d in range(1, 8):
        yd = lax.rem(y + d, 8)
        ypeer[d] = {"blk": x * NYL + lax.rem(yd, NYL), "neg": zbase + lax.div(yd, NYL) * 2 + core}
    xpeer = {}
    for d in range(1, 8):
        xd = lax.rem(x + d // 2, NX)
        xpeer[d] = {"blk": xd * NYL + yl, "neg": mpeer[1]["neg"] if d % 2 else neg}

    load_p = pltpu.make_async_copy(p_hbm.at[:, pl.ds(0, half)], pv.at[:, pl.ds(0, half)], lsem.at[0])
    load_r = pltpu.make_async_copy(p_hbm.at[:, pl.ds(half, half)], pv.at[:, pl.ds(half, half)], lsem.at[6])
    load_q = pltpu.make_async_copy(q_hbm, qv, lsem.at[1])
    load_own = pltpu.make_async_copy(own_hbm, own_ref, lsem.at[2])
    load_blk = pltpu.make_async_copy(blk_hbm, blk_ref, lsem.at[3])
    load_pos = pltpu.make_async_copy(pos_hbm, pos_ref, lsem.at[4])
    load_pick = pltpu.make_async_copy(pick_hbm, pick_ref, lsem.at[5])
    load_p.start()
    load_r.start()

    barrier = pltpu.get_barrier_semaphore()
    greet = [zpeer[4], mpeer[3], ypeer[4], after, before]
    greet += [zpeer[d] for d in ZORDER[1:]]
    greet += [ypeer[d] for d in ZORDER[1:]]
    greet += [xpeer[d] for d in (5, 4, 3, 2, 7, 6, 1)]
    for who in greet:
        pl.semaphore_signal(barrier, inc=1, device_id=who, device_id_type=MESH)
    load_own.start()
    load_blk.start()
    load_q.start()
    load_pos.start()
    load_pick.start()

    load_own.wait()
    load_blk.wait()
    srow = lax.broadcasted_iota(jnp.int32, (H * HB, rows), 0)
    owner = jnp.zeros_like(srow)
    place = jnp.zeros_like(srow)
    for h in range(H):
        owner = jnp.where(srow // HB == h, own_ref[:, h:h + 1], owner)
        place = jnp.where(srow // HB == h, blk_ref[:, h:h + 1], place)
    chosen = (owner == neg) & (place * HB + srow % HB == lax.broadcasted_iota(jnp.int32, srow.shape, 1))
    sel = chosen.astype(jnp.float32).astype(jnp.bfloat16)
    load_p.wait()
    fsend[0:SHARED, :] = nn(sel, pv[:, :half]).astype(jnp.bfloat16)
    load_r.wait()
    fsend[SHARED:, :] = nn(sel, pv[:, half:]).astype(jnp.bfloat16)
    pl.semaphore_wait(barrier, len(greet))

    def push(src, dst, sems, who):
        pltpu.make_async_remote_copy(
            src_ref=src, dst_ref=dst, send_sem=sems.at[0], recv_sem=sems.at[1],
            device_id=who, device_id_type=MESH,
        ).start()

    def all_of(ref, sems):
        return pltpu.make_async_remote_copy(
            src_ref=ref, dst_ref=ref, send_sem=sems.at[0], recv_sem=sems.at[1],
            device_id=after, device_id_type=MESH,
        )

    def arrive(ref, sems):
        all_of(ref, sems).wait_recv()

    def leave(ref, sems):
        all_of(ref, sems).wait_send()

    def part(ref, index):
        return ref.at[pl.ds(pl.multiple_of(index * HB, HB), HB), :]

    def scatter(buf, land, sems):
        for d in ZORDER:
            push(part(buf, zat[d]), land.at[d - 1], sems, zpeer[d])

    def gather(buf, sems):
        for d in ZORDER:
            push(part(buf, z), part(buf, z), sems, zpeer[d])

    def middle(buf, land, sems):
        for d in (3, 2, 1):
            push(buf, land.at[d - 1], sems, mpeer[d])

    def load_part(ref):
        return part(ref, z)[...].astype(jnp.float32)

    scatter(fsend, frecv, fr_s)
    push(pv, cv, c_s, after)

    scol = lax.broadcasted_iota(jnp.int32, (rows, H * HB), 1)
    owner_t = jnp.zeros_like(scol)
    place_t = jnp.zeros_like(scol)
    for h in range(H):
        owner_t = jnp.where(scol // HB == h, own_ref[:, h:h + 1], owner_t)
        place_t = jnp.where(scol // HB == h, blk_ref[:, h:h + 1], place_t)
    chosen_t = (owner_t == neg) & (
        place_t * HB + scol % HB == lax.broadcasted_iota(jnp.int32, scol.shape, 0)
    )
    sel_t = chosen_t.astype(jnp.float32).astype(jnp.bfloat16)
    load_q.wait()
    load_pos.wait()
    load_pick.wait()
    q = qv[...]
    qt[...] = q.T
    s0 = nn(pv[...], qt[...]) * scale
    hot = lax.broadcasted_iota(jnp.int32, s0.shape, 0) == pos_ref[...]
    spos = jnp.sum(jnp.where(hot, s0, 0.0), axis=0, keepdims=True)

    arrive(frecv, fr_s)
    fx[...] = part(fsend, z)[...] + sum(frecv[i] for i in range(NZ - 1))
    middle(fx, fxr, fx_s)
    arrive(fxr, fx_s)
    part(hv, z)[...] = (
        fx[...].astype(jnp.float32) + jnp.sum(fxr[...].astype(jnp.float32), axis=0)
    ).astype(jnp.bfloat16)
    gather(hv, fa_s)
    arrive(cv, c_s)
    s1 = nn(cv[...], qt[...]) * scale
    top01 = jnp.maximum(jnp.max(s0, axis=0, keepdims=True), jnp.max(s1, axis=0, keepdims=True))
    sum01 = jnp.sum(jnp.exp(s0 - top01), axis=0, keepdims=True) + jnp.sum(
        jnp.exp(s1 - top01), axis=0, keepdims=True
    )
    lane = lax.broadcasted_iota(jnp.int32, (H * HB, rows), 1)
    slot = lax.broadcasted_iota(jnp.int32, (H * HB, rows), 0) // HB
    first = jnp.where(lane < GQ, pick_ref[0:1, 0:1], pick_ref[1:2, 0:1])
    second = jnp.where(lane < GQ, pick_ref[0:1, 1:2], pick_ref[1:2, 1:2])
    picked = (slot == first) | (slot == second)
    arrive(frecv, fa_s)
    s2 = (nn(hv[0:SHARED, :], qt[:half, :]) + nn(hv[SHARED:, :], qt[half:, :])) * scale

    s2 = jnp.where(picked, s2, -jnp.inf)
    top = jnp.maximum(top01, jnp.max(s2, axis=0, keepdims=True))
    total = sum01 * jnp.exp(top01 - top) + jnp.sum(jnp.exp(s2 - top), axis=0, keepdims=True)
    lse = top + jnp.log(total)

    g2 = jnp.exp(s2 - lse).astype(jnp.bfloat16)
    gsend[0:SHARED, :] = (nn(g2, q[:, :half]) * scale).astype(jnp.bfloat16)
    gsend[SHARED:, :] = (nn(g2, q[:, half:]) * scale).astype(jnp.bfloat16)
    scatter(gsend, grecv, gr_s)

    l1[...] = lse - spos
    for d in ZORDER:
        push(l1, l1r.at[d - 1], l1_s, zpeer[d])

    g1 = jnp.exp(s1 - lse).astype(jnp.bfloat16)
    cgs[...] = (nn(g1, q) * scale).astype(jnp.bfloat16)
    push(cgs, cgr, k_s, before)

    g0 = (jnp.exp(s0 - lse) - hot.astype(jnp.float32)).astype(jnp.bfloat16)
    og[...] = nn(g0, q) * scale
    for side, lo in ((0, 0), (1, half)):
        out_ref[0, :, lo:lo + half] = (
            (
                tn(g0, pv[:, lo:lo + half])
                + tn(g1, cv[:, lo:lo + half])
                + tn(g2, hv[side * SHARED:(side + 1) * SHARED, :])
            )
            * scale
        ).astype(jnp.bfloat16)

    leave(frecv, fr_s)
    leave(fxr, fx_s)
    leave(frecv, fa_s)
    leave(cv, c_s)
    arrive(grecv, gr_s)
    gx[...] = (load_part(gsend) + jnp.sum(grecv[...].astype(jnp.float32), axis=0)).astype(jnp.bfloat16)
    middle(gx, gxr, gx_s)
    arrive(l1r, l1_s)
    l2[...] = l1[...] + jnp.sum(l1r[...], axis=0)
    for d in ZORDER:
        push(l2, l2r.at[d - 1], l2_s, ypeer[d])
    arrive(gxr, gx_s)
    part(gt, z)[...] = (
        gx[...].astype(jnp.float32) + jnp.sum(gxr[...].astype(jnp.float32), axis=0)
    ).astype(jnp.bfloat16)
    gather(gt, ga_s)
    arrive(l2r, l2_s)
    l3[...] = l2[...] + jnp.sum(l2r[...], axis=0)
    for d in range(1, 8):
        push(l3, l3r.at[d - 1], l3_s, xpeer[d])
    arrive(cgr, k_s)
    og[...] += cgr[...].astype(jnp.float32)
    arrive(l3r, l3_s)
    loss_ref[0, 0] = jnp.sum(l3[...] + jnp.sum(l3r[...], axis=0)) / n_all
    leave(grecv, gr_s)
    leave(gxr, gx_s)
    leave(grecv, ga_s)
    leave(cgr, k_s)
    leave(l1r, l1_s)
    leave(l2r, l2_s)
    leave(l3r, l3_s)
    arrive(grecv, ga_s)
    for side, lo in ((0, 0), (1, half)):
        shared = gt[side * SHARED:(side + 1) * SHARED, :]
        out_ref[1, :, lo:lo + half] = (og[:, lo:lo + half] + nn(sel_t, shared)).astype(jnp.bfloat16)


def body(queries, passages, positive, hard_owner, hard_block, hard_pick):
    rows, width = passages.shape
    n_all = rows * lax.axis_size("blk") * lax.axis_size("neg")
    bf = jnp.bfloat16
    f32 = jnp.float32
    any_space = pl.BlockSpec(memory_space=pl.ANY)
    vmem = pl.BlockSpec(memory_space=pltpu.VMEM)
    smem = pl.BlockSpec(memory_space=pltpu.SMEM)
    half = width // 2
    dma = pltpu.SemaphoreType.DMA
    loss, grads = pl.pallas_call(
        functools.partial(kernel, n_all),
        out_shape=(
            pltpu.SMEM((1, 1), f32),
            pltpu.VMEM((2, rows, width), bf),
        ),
        in_specs=[any_space] * 6,
        out_specs=(smem, vmem),
        scratch_shapes=[
            pltpu.VMEM((1, rows), jnp.int32),
            pltpu.VMEM(hard_owner.shape, jnp.int32),
            pltpu.VMEM(hard_block.shape, jnp.int32),
            pltpu.VMEM(hard_pick.shape, jnp.int32),
            pltpu.VMEM((width, rows), bf),
            pltpu.VMEM((rows, width), bf),
            pltpu.VMEM((rows, width), bf),
            pltpu.VMEM((rows, width), bf),
            pltpu.VMEM((2 * SHARED, half), bf),
            pltpu.VMEM((2 * SHARED, half), bf),
            pltpu.VMEM((NZ - 1, HB, half), bf),
            pltpu.VMEM((HB, half), bf),
            pltpu.VMEM((3, HB, half), bf),
            pltpu.VMEM((2 * SHARED, half), bf),
            pltpu.VMEM((NZ - 1, HB, half), bf),
            pltpu.VMEM((HB, half), bf),
            pltpu.VMEM((3, HB, half), bf),
            pltpu.VMEM((2 * SHARED, half), bf),
            pltpu.VMEM((rows, width), bf),
            pltpu.VMEM((rows, width), bf),
            pltpu.VMEM((rows, width), f32),
            pltpu.VMEM((1, rows), f32),
            pltpu.VMEM((7, 1, rows), f32),
            pltpu.VMEM((1, rows), f32),
            pltpu.VMEM((7, 1, rows), f32),
            pltpu.VMEM((1, rows), f32),
            pltpu.VMEM((7, 1, rows), f32),
            dma((7,)),
            dma((2,)),
            dma((2,)),
            dma((2,)),
            dma((2,)),
            dma((2,)),
            dma((2,)),
            dma((2,)),
            dma((2,)),
            dma((2,)),
            dma((2,)),
            dma((2,)),
        ],
        compiler_params=pltpu.CompilerParams(collective_id=0, has_side_effects=True),
        name="retriever",
    )(queries, passages, positive.reshape(1, rows), hard_owner, hard_block, hard_pick)
    return (loss[0, 0], grads[0], grads[1])


def solution(mesh):
    placed = (
        P(("blk", "neg"), None),
        P(("blk", "neg"), None),
        P(("blk", "neg")),
        P("blk", None),
        P("blk", None),
        P(("blk", "neg"), None),
    )
    return jax.shard_map(
        body,
        mesh=mesh,
        in_specs=placed,
        out_specs=(P(), P(("blk", "neg"), None), P(("blk", "neg"), None)),
        check_vma=False,
    )
```
